256 devices in a mesh: tile: 32 (over y, z), band: 8 (over x, core).
Axes of the slice: x: 4, y: 4, z: 8, core: 2. Of those that a mesh axis runs over, the one named last changes fastest.
Arguments:
- observed: float32 [96, 16384, 128], P('band', 'tile'), may hold values from 0 to 4
- weights: float32 [96, 16384, 128], P('band', 'tile'), may hold values from 0.2 to 6, as said below
- morphology: float32 [4, 16384, 128], P(None, 'tile'), may hold values from 0 to 1
- spectra: float32 [4, 96, 8192], P(None, 'band', 'tile'), may hold values from 0.2 to 2
- blend_blocks: int32 [32, 256], P('tile'), may hold values from 1 to 4, 512 in all within a row
- source_count: int32 [8192], P('tile'), may hold values from 1 to 4
- sent_blocks: int32 [32, 32, 4], P('tile'), may hold values from 0 to 512, as said below
- landing_blocks: int32 [32, 32, 4], P('tile'), may hold values from 0 to 512, as said below
Outputs:
- new_morphology: float32 [4, 16384, 128], P(None, 'tile')
- new_spectra: float32 [4, 96, 8192], P(None, 'band', 'tile')
- misfit: float32 [8192], P('tile')
The draws below stay inside these ranges and needn't reach their ends.
Inputs may be any that keep to these rules, and one draw needn't show every extreme that they name: `weights`: Positive. `sent_blocks`: entry [s, d, j] is a block of tile index s whose model margins a block of tile index d, or 512 for an empty slot; at most 4 live slots from one sender to one receiver, the live ones first; every sender fills all 4 slots to some receiver and every receiver gets all 4 from some sender; a block may appear in several slots. `landing_blocks`: entry [d, s, j] is the block of tile index d on which slot j from sender s lands, or 512 exactly where sent_blocks[s, d, j] is 512; several slots may land on one block.
All inputs are finite; a program needn't handle non-finite values.
Results may differ from the reference program's by a relative error of at most 0.0003.
Values sent between devices are 32-bit elements; how exact they have to be, the bound alone decides.
No kernel may reach another device: no remote copies, remote signals or barrier semaphores. Data moves between devices by JAX's collectives and lax.ppermute only.
A program may use at most 128 MiB of HBM per device.

```python
import math
import jax
import jax.numpy as jnp
import numpy as np
from jax import lax

PIX = 128
SOURCES = 4
CAP = 4
ITERS = 2
BLK_DEV = 512
BLEND_DEV = 256
CHAN = 96
BLOCKS = 16384
BLENDS = 8192
N_TILE = 32


def link_tables(key):
    base = jax.random.fold_in(key, 7)
    count_key, from_key, land_key = jax.random.split(base, 3)
    counts = jax.random.randint(count_key, (N_TILE, N_TILE), 0, CAP + 1)
    rows = jnp.arange(N_TILE)
    successor = rows[None, :] == (rows[:, None] + 1) % N_TILE
    counts = jnp.where(successor, CAP, counts)
    slot_index = jnp.arange(CAP)
    live_from = slot_index[None, None, :] < counts[:, :, None]
    sent_rows = jnp.where(live_from, jax.random.randint(from_key, (N_TILE, N_TILE, CAP), 0, BLK_DEV), BLK_DEV)
    land_rows = jnp.where(jnp.transpose(live_from, (1, 0, 2)), jax.random.randint(land_key, (N_TILE, N_TILE, CAP), 0, BLK_DEV), BLK_DEV)
    return (sent_rows.astype(jnp.int32), land_rows.astype(jnp.int32))


def draw_sent_blocks(key, part):
    return link_tables(key)[0]


def draw_landing_blocks(key, part):
    return link_tables(key)[1]


def draw_weights(key, part):
    ramp = jnp.exp(jnp.log(3.0) * jnp.arange(CHAN, dtype=jnp.float32) / max(CHAN - 1, 1))
    noise = jnp.exp(jax.random.uniform(key, (CHAN, BLOCKS, PIX), jnp.float32, jnp.log(0.5), jnp.log(2.0)))
    return (ramp[:, None, None] * noise).astype(jnp.float32)


def with_ends(values, rng, least, top_value):
    index_at = [jax.random.randint(jax.random.fold_in(rng, axis), (), 0, length) for axis, length in enumerate(values.shape)]
    main_axis = values.shape.index(max(values.shape))
    next_to = index_at[:main_axis] + [(index_at[main_axis] + 1) % values.shape[main_axis]] + index_at[main_axis + 1:]
    return values.at[tuple(index_at)].set(least).at[tuple(next_to)].set(top_value)


def steps_of(rng, extent, pieces, least, top_value):
    def one(dim, blocks):
        steps = jax.random.uniform(jax.random.fold_in(jax.random.fold_in(rng, 6), dim), (blocks,), jnp.float32, least / len(pieces), top_value / len(pieces))
        return jnp.repeat(jnp.exp(steps), extent[dim] // blocks).reshape((-1,) + (1,) * (len(extent) - dim - 1))

    loudness = one(*pieces[0])
    for cut in pieces[1:]:
        loudness = loudness * one(*cut)
    return loudness


def length_profile(count, total, limit, skew):
    weights = [(1 << 20) // math.isqrt(standing ** skew) + 1 for standing in range(2, count + 1)]
    surplus, holding = total - limit - (count - 1), [1] * (count - 1)
    while surplus > 0:
        movable = [i for i in range(count - 1) if holding[i] < limit]
        pool, remaining = sum([weights[i] for i in movable]), surplus
        for i in movable:
            addition = min(limit - holding[i], max(1, remaining * weights[i] // pool), surplus)
            holding[i] = holding[i] + addition
            surplus = surplus - addition
    return np.array([limit] + holding)


def ragged(stream_key, amount, total, most, slope):
    if amount == 2:
        one = jax.random.randint(stream_key, (), max(1, total - most), min(most, total - 1) + 1)
        return jnp.stack([one, total - one])
    lengths = jnp.asarray(length_profile(amount, total, most, slope), jnp.int32)
    pairs = (amount - 1) // 2
    donor, sink = lengths[1:1 + 2 * pairs:2], lengths[2:2 + 2 * pairs:2]
    slack = jnp.minimum(donor - 1, most - sink)
    passed = jax.random.randint(jax.random.fold_in(stream_key, 1), (pairs,), 0, 1 << 20) % (slack + 1)
    lengths = lengths.at[1:1 + 2 * pairs:2].set(donor - passed).at[2:2 + 2 * pairs:2].set(sink + passed)
    return lengths[jax.random.permutation(jax.random.fold_in(stream_key, 2), amount)]


def setup_inputs(seed: int = 0) -> dict:
    seeds = jax.random.split(jax.random.key(seed), 9)
    observed = jnp.clip(4.0 * jax.random.uniform(seeds[0], (CHAN, BLOCKS, PIX), jnp.float32) ** steps_of(seeds[0], (CHAN, BLOCKS, PIX), ((0, 8), (1, 32)), -0.2, 0.2), 0.0, 4.0)
    weights = draw_weights(jax.random.fold_in(seeds[8], 71), 0)
    morphology = jnp.clip(1.0 * jax.random.uniform(seeds[2], (SOURCES, BLOCKS, PIX), jnp.float32) ** steps_of(seeds[2], (SOURCES, BLOCKS, PIX), ((1, 32),), -0.2, 0.2), 0.0, 1.0)
    spectra = jnp.clip(jnp.exp(math.log(2.0) - 2.3025851 * jax.random.uniform(seeds[3], (SOURCES, CHAN, BLENDS), jnp.float32) ** steps_of(seeds[3], (SOURCES, CHAN, BLENDS), ((1, 8), (2, 32)), -0.2, 0.2)), 0.2, 2.0)
    blend_blocks = jax.vmap(lambda own: ragged(own, BLEND_DEV, BLK_DEV, 4, 1))(jax.random.split(seeds[4], N_TILE)).reshape((N_TILE, BLEND_DEV)).astype(jnp.int32)
    source_count = with_ends(jax.random.randint(seeds[5], (BLENDS,), 1, SOURCES + 1), jax.random.fold_in(seeds[5], 1), 1, SOURCES).astype(jnp.int32)
    sent_blocks = draw_sent_blocks(jax.random.fold_in(seeds[8], 71), 0)
    landing_blocks = draw_landing_blocks(jax.random.fold_in(seeds[8], 71), 0)
    return {"observed": observed, "weights": weights, "morphology": morphology, "spectra": spectra, "blend_blocks": blend_blocks, "source_count": source_count, "sent_blocks": sent_blocks, "landing_blocks": landing_blocks}


HIGH = lax.Precision.HIGHEST


def reference(observed, weights, morphology, spectra, blend_blocks, source_count, sent_blocks, landing_blocks):
    block_ends = jnp.cumsum(blend_blocks, axis=1)
    position = jnp.arange(BLK_DEV, dtype=jnp.int32)
    local_blend = jnp.sum((block_ends[:, None, :] <= position[None, :, None]).astype(jnp.int32), axis=2)
    tile_base = jnp.arange(N_TILE, dtype=jnp.int32)
    block_blend = (local_blend + BLEND_DEV * tile_base[:, None]).reshape(-1).astype(jnp.int32)
    alive_slots = (jnp.arange(SOURCES, dtype=jnp.int32)[:, None] < source_count[None, :]).astype(jnp.float32)
    alive_blocks = alive_slots[:, block_blend]
    shape_now = morphology * alive_blocks[:, :, None]
    color_now = spectra * alive_slots[:, None, :]
    source_live = sent_blocks < BLK_DEV
    source_global = jnp.where(source_live, tile_base[:, None, None] * BLK_DEV + sent_blocks, BLOCKS).reshape(-1).astype(jnp.int32)
    landing_turned = jnp.transpose(landing_blocks, (1, 0, 2))
    target_global = jnp.where(landing_turned < BLK_DEV, tile_base[None, :, None] * BLK_DEV + landing_turned, BLOCKS).reshape(-1).astype(jnp.int32)
    misfit = jnp.zeros((BLENDS,), jnp.float32)
    for iteration in range(ITERS):
        color_blocks = color_now[:, :, block_blend]
        own_model = jnp.einsum('kcb,kbp->cbp', color_blocks, shape_now, precision=HIGH)
        incoming = jnp.take(own_model, source_global, axis=1, mode="fill", fill_value=0.0)
        full_model = own_model.at[:, target_global].add(incoming, mode="drop")
        residual = full_model - observed
        weighted = weights * residual
        misfit = jax.ops.segment_sum(jnp.sum(weighted * residual, axis=(0, 2)), block_blend, num_segments=BLENDS)
        returning = jnp.take(weighted, target_global, axis=1, mode="fill", fill_value=0.0)
        adjoint = weighted.at[:, source_global].add(returning, mode="drop")
        grad_shape = jnp.einsum('kcb,cbp->kbp', color_blocks, adjoint, precision=HIGH)
        per_block = jnp.einsum('kbp,cbp->bkc', shape_now, adjoint, precision=HIGH)
        grad_color = jnp.transpose(jax.ops.segment_sum(per_block, block_blend, num_segments=BLENDS), (1, 2, 0))
        color_power = jnp.sum(color_now * color_now, axis=1)
        step_shape = 1.0 / (1.0 + color_power[:, block_blend])
        shape_power = jax.ops.segment_sum(jnp.sum(shape_now * shape_now, axis=2).T, block_blend, num_segments=BLENDS).T
        step_color = 1.0 / (1.0 + shape_power)
        shape_next = jnp.maximum(shape_now - step_shape[:, :, None] * grad_shape, 0.0) * alive_blocks[:, :, None]
        color_now = jnp.maximum(color_now - step_color[:, None, :] * grad_color, 0.0) * alive_slots[:, None, :]
        shape_now = shape_next
    return shape_now, color_now, misfit
```

```python
import functools

import jax
import jax.numpy as jnp
from jax import lax
from jax.experimental import pallas as pl
from jax.experimental.pallas import tpu as pltpu
from jax.sharding import PartitionSpec as P


ITERS = 2
F32 = jnp.float32
BF16 = jnp.bfloat16
HIGH = lax.Precision.HIGHEST
KPAD = 16
ROWS = 16
SMALL = 8 << 20
EXTRA = 8
NN = (((1,), (0,)), ((), ()))
NT = (((1,), (1,)), ((), ()))
TN = (((0,), (0,)), ((), ()))


def halves(x):
    hi = x.astype(BF16)
    return hi, (x - hi.astype(F32)).astype(BF16)


def pick(onehot, x, dims=NN):
    n = x.shape[1]
    both = jnp.concatenate(halves(x), axis=1)
    y = lax.dot_general(onehot, both, dims, preferred_element_type=F32)
    return y[:, :n] + y[:, n:]


def exact(a, b, dims):
    return lax.dot_general(a, b, dims, precision=HIGH, preferred_element_type=F32)


def iota(shape, dim):
    return lax.broadcasted_iota(jnp.int32, shape, dim)


def hot(mask):
    return jnp.where(mask, 1.0, 0.0).astype(BF16)


def slot_row(idx):
    cap, peers = idx.shape
    slots = cap * peers
    spread = hot(iota((peers, slots), 1) % peers == iota((peers, slots), 0))
    hi, lo = halves(idx.astype(F32))
    wide = jnp.dot(hi, spread, preferred_element_type=F32) + jnp.dot(
        lo, spread, preferred_element_type=F32
    )
    own = iota((cap, slots), 1) // peers == iota((cap, slots), 0)
    return jnp.sum(jnp.where(own, wide, 0.0), axis=0, keepdims=True)


def slot_column(idx):
    row = slot_row(idx)
    n = row.shape[1]
    return jnp.sum(jnp.where(iota((n, n), 0) == iota((n, n), 1), row, 0.0), axis=1, keepdims=True)


def slots_by_block(idx, blocks):
    slots = idx.shape[0] * idx.shape[1]
    return hot(slot_column(idx) == iota((slots, blocks), 1).astype(F32))


def blocks_by_slot(idx, blocks):
    slots = idx.shape[0] * idx.shape[1]
    return hot(slot_row(idx) == iota((blocks, slots), 0).astype(F32))


def membership_of(lengths, blocks, first=0):
    n = lengths.shape[1]
    upto = hot(iota((n, n), 0) <= iota((n, n), 1))
    rows = jnp.broadcast_to(lengths.astype(F32), (8, n))
    ends = lax.dot_general(rows.astype(BF16), upto, NN, preferred_element_type=F32)[:1]
    starts = ends - lengths.astype(F32)
    position = (iota((blocks, n), 0) + first).astype(F32)
    return hot((position >= starts) & (position < ends))


def band_place():
    me = lax.axis_index("band")
    return me // 2, me % 2


def write_message(out, leaving, colours):
    peers = out.shape[0] // ROWS
    lane = iota((peers, 128), 1)
    out[...] = jnp.zeros(out.shape, F32)
    for k2 in range(2):
        for j in range(4):
            out[pl.ds(k2 * 4 + j, peers, stride=ROWS), :] = leaving[k2][j * peers : (j + 1) * peers]
    for jj in range(2):
        low = colours[jj * peers : (jj + 1) * peers]
        high = colours[(jj + 2) * peers : (jj + 3) * peers]
        out[pl.ds(8 + jj, peers, stride=ROWS), :] = jnp.where(lane < 64, low, high)


def colour_table(member, colour):
    twice = jnp.concatenate([colour, colour], axis=0)
    hi, lo = halves(twice)
    mid = lax.dot_general(member, hi, NT, preferred_element_type=F32)
    return mid + lax.dot_general(member, lo, NT, preferred_element_type=F32)


def started(copies):
    for c in copies:
        c.start()
    return copies


def start_kernel(
    morph_far,
    spectra_far,
    lengths_far,
    counts_far,
    sent_far,
    land_far,
    own,
    other,
    colour,
    alive,
    table,
    ablk,
    lengths,
    sent,
    land,
    message_far,
    morph,
    spectra,
    counts,
    message,
    sems,
):
    _, h = band_place()
    near = (lengths, counts, spectra, sent, morph, land)
    far = (lengths_far, counts_far, spectra_far, sent_far, morph_far, land_far)
    arrivals = started(
        [pltpu.make_async_copy(f, n, sems.at[i]) for i, (f, n) in enumerate(zip(far, near))]
    )
    for c in arrivals[:3]:
        c.wait()
    blocks = own.shape[1]
    blends = colour.shape[1]
    channels = spectra.shape[0]
    member = membership_of(lengths[...], blocks)
    rel = iota((8, blends), 0)
    absolute = jnp.where(rel < 4, rel ^ (2 * h), 8)
    live = jnp.where(absolute < counts[...], 1.0, 0.0).astype(F32)
    alive[...] = live
    colour[...] = jnp.zeros(colour.shape, F32)
    for c in range(channels):
        for k in range(4):
            colour[pl.ds(k * KPAD + c, 1), :] = spectra[c, pl.ds(k ^ (2 * h), 1), :]
    for k in range(4):
        at = pl.ds(k * KPAD, KPAD)
        colour[at, :] = colour[at, :] * live[k : k + 1]
    table[...] = colour_table(member, colour[...])
    wide = jnp.concatenate([live, jnp.zeros((120, blends), F32)], axis=0).astype(BF16)
    ab = lax.dot_general(member, wide, NT, preferred_element_type=F32)
    ablk[...] = ab
    for c in arrivals[3:]:
        c.wait()
    for k2 in range(2):
        own[k2] = morph[k2 ^ (2 * h)] * ab[:, k2 : k2 + 1]
        other[k2] = morph[(k2 + 2) ^ (2 * h)] * ab[:, k2 + 2 : k2 + 3]
    take = slots_by_block(sent[0], blocks)
    write_message(message, [pick(take, own[0]), pick(take, own[1])], pick(take, table[...]))
    pltpu.sync_copy(message, message_far)


def model_kernel(table, own, other, observed_far, out_far, observed, out, sem_in, sem_out):
    channels, blocks, _ = observed.shape

    def there(t):
        return slice(None), pl.ds(pl.multiple_of(t * 128, 128), 128)

    def arrival(t):
        return pltpu.make_async_copy(observed_far.at[there(t)], observed.at[there(t)], sem_in.at[t])

    def leaving(t):
        return pltpu.make_async_copy(out.at[there(t)], out_far.at[there(t)], sem_out.at[t])

    for t in range(blocks // 128):
        arrival(t).start()

    def tile(t, carry):
        arrival(t).wait()
        rows = pl.ds(pl.multiple_of(t * 128, 128), 128)
        cb = table[rows, :]
        sh = [own[0, rows, :], own[1, rows, :], other[0, rows, :], other[1, rows, :]]
        for c in range(channels):
            m = sh[0] * cb[:, c : c + 1]
            for k in range(1, 4):
                m = m + sh[k] * cb[:, k * KPAD + c : k * KPAD + c + 1]
            out[c, rows, :] = m - observed[c, rows, :]
        leaving(t).start()
        return carry

    lax.fori_loop(0, blocks // 128, tile, 0)
    for t in range(blocks // 128):
        leaving(t).wait()


def link_kernel(
    last,
    mine,
    partner,
    resid_far,
    weights_far,
    land,
    wout_far,
    keep,
    send,
    miss,
    shs,
    back,
    sbs,
    ssb,
    macc,
    resid,
    weights,
    wout,
    sem_r,
    sem_w,
    sem_out,
):
    channels, blocks, pixels = resid.shape
    came_r = [pltpu.make_async_copy(resid_far.at[c], resid.at[c], sem_r.at[c]) for c in range(channels)]
    came_w = [
        pltpu.make_async_copy(weights_far.at[c], weights.at[c], sem_w.at[c]) for c in range(channels)
    ]
    gone = [pltpu.make_async_copy(wout.at[c], wout_far.at[c], sem_out.at[c]) for c in range(channels)]
    for c in range(channels):
        came_r[c].start()
        came_w[c].start()
    peers = land.shape[2]
    slots = 4 * peers
    sbs[...] = blocks_by_slot(land[0], blocks)
    ssb[...] = slots_by_block(land[0], blocks)
    for k2 in range(2):
        for j in range(4):
            rows = pl.ds(j * peers, peers)
            shs[k2, rows, :] = mine[pl.ds(k2 * 4 + j, peers, stride=ROWS), :]
            shs[k2 + 2, rows, :] = partner[pl.ds(k2 * 4 + j, peers, stride=ROWS), :]
    ci = [mine[pl.ds(8 + jj, peers, stride=ROWS), :] for jj in range(2)]
    lane = iota((peers, 128), 1)
    bc = [jnp.zeros((peers, 128), F32) for _ in range(2)]
    for c in range(channels):
        parts = []
        for j in range(4):
            rows = pl.ds(j * peers, peers)
            at = c + (64 if j >= 2 else 0)
            m = shs[0, rows, :] * ci[j % 2][:, at : at + 1]
            for k in range(1, 4):
                col = at + k * KPAD
                m = m + shs[k, rows, :] * ci[j % 2][:, col : col + 1]
            parts.append(m)
        both = jnp.concatenate(halves(jnp.concatenate(parts, axis=0)), axis=1)
        landed = jnp.zeros((slots, 2 * pixels), F32)
        came_r[c].wait()
        came_w[c].wait()
        for q in range(blocks // 128):
            rows = pl.ds(q * 128, 128)
            y = jnp.dot(sbs[rows, :], both, preferred_element_type=F32)
            x = resid[c, rows, :] + (y[:, :pixels] + y[:, pixels:])
            wt = weights[c, rows, :] * x
            wout[c, rows, :] = wt
            if last:
                term = wt * x
                macc[rows, :] = term if c == 0 else macc[rows, :] + term
            wboth = jnp.concatenate(halves(wt), axis=1)
            landed = landed + jnp.dot(ssb[:, rows], wboth, preferred_element_type=F32)
        gone[c].start()
        landed = landed[:, :pixels] + landed[:, pixels:]
        for j in range(4):
            rows = pl.ds(j * peers, peers)
            at = c + (64 if j >= 2 else 0)
            ld = landed[j * peers : (j + 1) * peers]
            for k in range(4):
                col = at + k * KPAD
                term = ci[j % 2][:, col : col + 1] * ld
                back[k, rows, :] = term if c == 0 else back[k, rows, :] + term
                r = jnp.sum(shs[k, rows, :] * ld, axis=1, keepdims=True)
                bc[j % 2] = jnp.where(lane == col, r, bc[j % 2])
    keep[...] = jnp.zeros(keep.shape, F32)
    send[...] = jnp.zeros(send.shape, F32)
    for k2 in range(2):
        for j in range(4):
            rows = pl.ds(j * peers, peers)
            keep[pl.ds(k2 * 4 + j, peers, stride=ROWS), :] = back[k2, rows, :]
            send[pl.ds(k2 * 4 + j, peers, stride=ROWS), :] = back[k2 + 2, rows, :]
    for jj in range(2):
        keep[pl.ds(8 + jj, peers, stride=ROWS), :] = bc[jj]
    if last:
        miss[...] = exact(jnp.ones((8, pixels), F32), macc[...], NT)
    else:
        miss[...] = jnp.zeros(miss.shape, F32)
    for c in range(channels):
        gone[c].wait()


def grad_kernel(
    table, own, other, wgt_far, colour, lengths, miss, after, keep, send, per_block, wgt, sems
):
    channels, blocks, _ = wgt.shape

    def arrival(t):
        there = slice(None), pl.ds(pl.multiple_of(t * 128, 128), 128)
        return pltpu.make_async_copy(wgt_far.at[there], wgt.at[there], sems.at[t])

    for t in range(blocks // 128):
        arrival(t).start()
    lane = iota((128, 128), 1)
    quarter = blocks // 4

    def colours(t, carry):
        arrival(t).wait()
        rows = pl.ds(pl.multiple_of(t * 128, 128), 128)
        sh = [own[0, rows, :], own[1, rows, :], other[0, rows, :], other[1, rows, :]]
        pb = jnp.zeros((128, 128), F32)
        for c in range(channels):
            wt = wgt[c, rows, :]
            for k in range(4):
                r = jnp.sum(sh[k] * wt, axis=1, keepdims=True)
                pb = jnp.where(lane == k * KPAD + c, r, pb)
        per_block[rows, :] = pb
        return carry

    lax.fori_loop(0, blocks // 128, colours, 0)

    def shapes(t, carry):
        q, inside = t // 2, pl.multiple_of((t % 2) * 64, 64)
        rows = pl.ds(pl.multiple_of(t * 64, 64), 64)
        cb = table[rows, :]
        gs = [None] * 4
        for c in range(channels):
            wt = wgt[c, rows, :]
            for k in range(4):
                term = cb[:, k * KPAD + c : k * KPAD + c + 1] * wt
                gs[k] = term if c == 0 else gs[k] + term
        for k2 in range(2):
            keep[q, pl.ds(k2 * quarter + inside, 64), :] = gs[k2]
            send[q, pl.ds(k2 * quarter + inside, 64), :] = gs[k2 + 2]
        return carry

    lax.fori_loop(0, blocks // 64, shapes, 0)
    member = membership_of(lengths[...], blocks)
    sq = colour[...] * colour[...]
    rows8 = iota((8, sq.shape[1]), 0)
    power = jnp.zeros((8, sq.shape[1]), F32)
    for k in range(4):
        total = jnp.sum(sq[k * KPAD : (k + 1) * KPAD], axis=0, keepdims=True)
        power = jnp.where(rows8 == k, total, power)
    hi, lo = halves(power)
    wide = lax.dot_general(hi, member, NT, preferred_element_type=F32) + lax.dot_general(
        lo, member, NT, preferred_element_type=F32
    )
    for q in range(4):
        w = wide[:, q * quarter : (q + 1) * quarter]
        m = miss[0:1, q * quarter : (q + 1) * quarter]
        r = iota((8, quarter), 0)
        first = jnp.where(r == 0, m, jnp.where(r == 1, w[0:1], jnp.where(r == 2, w[1:2], 0.0)))
        second = jnp.where(r == 0, m, jnp.where(r == 1, w[2:3], jnp.where(r == 2, w[3:4], 0.0)))
        keep[q, pl.ds(2 * quarter, EXTRA), :] = first
        send[q, pl.ds(2 * quarter, EXTRA), :] = second


def merge_kernel(arrived, keep, came, sent, p0, p1, p2, p3, scat):
    x, _ = band_place()
    peers = sent.shape[2]
    quarter = (p0.shape[0] - EXTRA) // 2
    blocks = 4 * quarter
    put = blocks_by_slot(sent[0], blocks)
    for k2 in range(2):
        rows = [arrived[pl.ds(k2 * 4 + j, peers, stride=ROWS), :] for j in range(4)]
        scat[k2] = pick(put, jnp.concatenate(rows, axis=0))
    for step, out in enumerate((p0, p1, p2, p3)):
        q = lax.rem(x + step, 4)
        out[...] = keep[q] + came[q]
        for k2 in range(2):
            at = pl.ds(pl.multiple_of(q * quarter, quarter), quarter)
            out[pl.ds(k2 * quarter, quarter), :] += scat[k2, at, :]


def colour_kernel(
    last, arrived, sent, per_block, lengths, own, other, colour, alive, *outs
):
    if last:
        out, fresh = outs
    else:
        fresh, table = outs
    blocks = per_block.shape[0]
    peers = sent.shape[2]
    member = membership_of(lengths[...], blocks)
    put = blocks_by_slot(sent[0], blocks)
    lane = iota((peers, 128), 1)
    rows = []
    for j in range(4):
        row = arrived[pl.ds(8 + j % 2, peers, stride=ROWS), :]
        rows.append(jnp.where((lane < 64) == (j < 2), row, 0.0))
    total = per_block[...] + pick(put, jnp.concatenate(rows, axis=0))
    hi, lo = halves(total)
    grad = lax.dot_general(hi, member, TN, preferred_element_type=F32) + lax.dot_general(
        lo, member, TN, preferred_element_type=F32
    )
    grad = grad[:64] + grad[64:]
    ones = jnp.ones((8, own.shape[2]), F32)
    for k in range(4):
        s = own[k] if k < 2 else other[k - 2]
        by_block = exact(ones, s * s, NT)
        hi, lo = halves(by_block)
        power = lax.dot_general(hi, member, NN, preferred_element_type=F32) + lax.dot_general(
            lo, member, NN, preferred_element_type=F32
        )
        step = 1.0 / (1.0 + power[:1])
        at = pl.ds(k * KPAD, KPAD)
        new = (
            jnp.maximum(colour[at, :] - step * grad[k * KPAD : (k + 1) * KPAD], 0.0)
            * alive[k : k + 1, :]
        )
        fresh[at, :] = new
    if last:
        _, h = band_place()
        for c in range(out.shape[0]):
            for k in range(4):
                out[c, pl.ds(k ^ (2 * h), 1), :] = fresh[pl.ds(k * KPAD + c, 1), :]
    else:
        table[...] = colour_table(member, fresh[...])


def update_kernel(p0, r1, r2, r3, own, ablk, out):
    x, _ = band_place()
    quarter = (p0.shape[0] - EXTRA) // 2
    total = p0[...] + r1[...] + r2[...] + r3[...]
    at = pl.ds(pl.multiple_of(x * quarter, quarter), quarter)
    ab = ablk[at, :]
    eye = iota((quarter, quarter), 0) == iota((quarter, quarter), 1)
    for k2 in range(2):
        row = total[2 * quarter + 1 + k2 : 2 * quarter + 2 + k2]
        power = jnp.sum(jnp.where(eye, row, 0.0), axis=1, keepdims=True)
        step = 1.0 / (1.0 + power)
        g = total[k2 * quarter : (k2 + 1) * quarter]
        out[pl.ds(k2 * quarter, quarter), :] = (
            jnp.maximum(own[k2, at, :] - step * g, 0.0) * ab[:, k2 : k2 + 1]
        )
    out[pl.ds(2 * quarter, EXTRA), :] = total[2 * quarter :]


def leave_kernel(n0, r1, r2, r3, table, sent, pair, message_far, message):
    x, _ = band_place()
    quarter = (n0.shape[0] - EXTRA) // 2
    for step, piece in enumerate((n0, r1, r2, r3)):
        q = lax.rem(x + 4 - step, 4)
        at = pl.ds(pl.multiple_of(q * quarter, quarter), quarter)
        for k2 in range(2):
            pair[k2, at, :] = piece[pl.ds(k2 * quarter, quarter), :]
    take = slots_by_block(sent[0], 4 * quarter)
    write_message(message, [pick(take, pair[0]), pick(take, pair[1])], pick(take, table[...]))
    pltpu.sync_copy(message, message_far)


def finish_kernel(n0, r1, r2, r3, m0, m1, m2, m3, lengths, shape, misfit):
    x, h = band_place()
    quarter = (n0.shape[0] - EXTRA) // 2
    total = jnp.zeros((8, lengths.shape[1]), F32)
    for step, (mine, theirs) in enumerate(((n0, m0), (r1, m1), (r2, m2), (r3, m3))):
        q = lax.rem(x + 4 - step, 4)
        at = pl.ds(pl.multiple_of(q * quarter, quarter), quarter)
        for k2 in range(2):
            shape[k2 + 2 * h, at, :] = mine[pl.ds(k2 * quarter, quarter), :]
            shape[k2 + 2 * (1 - h), at, :] = theirs[pl.ds(k2 * quarter, quarter), :]
        ms = mine[pl.ds(2 * quarter, EXTRA), :]
        part = membership_of(lengths[...], quarter, q * quarter)
        hi, lo = halves(ms)
        total = total + lax.dot_general(hi, part, NN, preferred_element_type=F32)
        total = total + lax.dot_general(lo, part, NN, preferred_element_type=F32)
    misfit[...] = total[:1]


def call(kernel, outs, args, scratch=(), limit=54_000_000, cost=3e6, far_in=(), far_out=()):
    many = isinstance(outs, list)
    shapes = [
        s if isinstance(s, jax.ShapeDtypeStruct) else jax.ShapeDtypeStruct(s, F32)
        for s in (outs if many else [outs])
    ]
    near = pl.BlockSpec(memory_space=pltpu.VMEM)
    far = pl.BlockSpec(memory_space=pltpu.HBM)
    got = pl.pallas_call(
        kernel,
        out_shape=shapes,
        in_specs=[far if i in far_in else near for i in range(len(args))],
        out_specs=[far if i in far_out else near for i in range(len(shapes))],
        scratch_shapes=list(scratch),
        compiler_params=pltpu.CompilerParams(vmem_limit_bytes=limit),
        cost_estimate=pl.CostEstimate(flops=0, bytes_accessed=int(cost), transcendentals=0),
    )(*args)
    return got if many else got[0]


def on_device(
    observed, weights, morphology, spectra, blend_blocks, source_count, sent_blocks, landing_blocks
):
    channels, blocks, pixels = observed.shape
    spectra = spectra.transpose(1, 0, 2)
    sent_blocks = sent_blocks.transpose(0, 2, 1)
    landing_blocks = landing_blocks.transpose(0, 2, 1)
    blends = spectra.shape[2]
    peers = sent_blocks.shape[2]
    slots = 4 * peers
    quarter = blocks // 4
    piece = (2 * quarter + EXTRA, pixels)
    pair = (2, blocks, pixels)
    message = (peers * ROWS, pixels)
    band = lax.axis_size("band")

    def over_core(v):
        return lax.ppermute(v, "band", [(i, i ^ 1) for i in range(band)])

    def over_x(v, step):
        return lax.ppermute(v, "band", [(i, (i + 2 * step) % band) for i in range(band)])

    def over_tile(v):
        v = v.reshape(peers, ROWS, pixels)
        return lax.all_to_all(v, "tile", 0, 0, tiled=True).reshape(message)

    counts = source_count.reshape(1, blends)
    colour_rows = (4 * KPAD, blends)
    table_rows = (blocks, 128)

    def kept(v):
        return jax.ShapeDtypeStruct(v.shape, v.dtype)

    def dma(n):
        return pltpu.SemaphoreType.DMA((n,))

    cube = pltpu.VMEM(observed.shape, F32)
    own, other, colour, alive, table, ablk, lengths, sent, land, leaving = call(
        start_kernel,
        [
            pair,
            pair,
            colour_rows,
            (8, blends),
            table_rows,
            table_rows,
            kept(blend_blocks),
            kept(sent_blocks),
            kept(landing_blocks),
            message,
        ],
        (morphology, spectra, blend_blocks, counts, sent_blocks, landing_blocks),
        scratch=(
            pltpu.VMEM(morphology.shape, F32),
            pltpu.VMEM(spectra.shape, F32),
            pltpu.VMEM(counts.shape, jnp.int32),
            pltpu.VMEM(message, F32),
            dma(6),
        ),
        limit=67_043_328,
        far_in=range(6),
        far_out=(9,),
    )
    for iteration in range(ITERS):
        last = iteration == ITERS - 1
        mine = over_tile(leaving)
        resid = call(
            model_kernel,
            observed.shape,
            (table, own, other, observed),
            scratch=(cube, cube, dma(blocks // 128), dma(blocks // 128)),
            cost=16e6,
            far_in=(3,),
            far_out=(0,),
        )
        mine, resid = lax.optimization_barrier((mine, resid))
        partner = over_core(mine)
        wgt, bkeep, bsend, miss = call(
            functools.partial(link_kernel, last),
            [observed.shape, message, message, (8, blocks)],
            (mine, partner, resid, weights, land),
            scratch=(
                pltpu.VMEM((4, slots, pixels), F32),
                pltpu.VMEM((4, slots, pixels), F32),
                pltpu.VMEM((blocks, slots), BF16),
                pltpu.VMEM((slots, blocks), BF16),
                pltpu.VMEM((blocks, pixels), F32),
                cube,
                cube,
                cube,
                dma(channels),
                dma(channels),
                dma(channels),
            ),
            cost=14e6,
            far_in=(2, 3),
            far_out=(0,),
        )
        returning = bkeep + over_core(bsend)
        back = over_tile(returning)
        gkeep, gsend, per_block = call(
            grad_kernel,
            [(4,) + piece, (4,) + piece, table_rows],
            (table, own, other, wgt, colour, lengths, miss, returning),
            scratch=(cube, dma(blocks // 128)),
            cost=30e6,
            far_in=(3, 7),
        )
        gcame = over_core(gsend)
        p0, p1, p2, p3 = call(
            merge_kernel,
            [piece] * 4,
            (back, gkeep, gcame, sent),
            scratch=(pltpu.VMEM(pair, F32),),
            limit=SMALL,
        )
        r1, r2, r3 = (over_x(v, s) for s, v in ((1, p1), (2, p2), (3, p3)))
        colour_args = (back, sent, per_block, lengths, own, other, colour, alive)
        if last:
            new_colour = call(
                functools.partial(colour_kernel, True),
                (channels, 4, blends),
                colour_args,
                scratch=(pltpu.VMEM(colour_rows, F32),),
                limit=SMALL,
                cost=8e6,
            )
        else:
            colour, table = call(
                functools.partial(colour_kernel, False),
                [colour_rows, table_rows],
                colour_args,
                limit=SMALL,
                cost=8e6,
            )
        n0 = call(update_kernel, piece, (p0, r1, r2, r3, own, ablk), limit=SMALL)
        n1, n2, n3 = (over_x(n0, s) for s in (1, 2, 3))
        if not last:
            own, leaving = call(
                leave_kernel, [pair, message], (n0, n1, n2, n3, table, sent),
                scratch=(pltpu.VMEM(message, F32),),
                limit=SMALL,
                far_out=(1,),
            )
            other = over_core(own)
    m0, m1, m2, m3 = (over_core(v) for v in (n0, n1, n2, n3))
    shape, misfit = call(
        finish_kernel,
        [morphology.shape, (1, blends)],
        (n0, n1, n2, n3, m0, m1, m2, m3, lengths),
        limit=SMALL,
    )
    return shape, new_colour.transpose(1, 0, 2), misfit.reshape(blends)


def solution(mesh):
    return jax.shard_map(
        on_device,
        mesh=mesh,
        in_specs=(
            P("band", "tile", None),
            P("band", "tile", None),
            P(None, "tile", None),
            P(None, "band", "tile"),
            P("tile", None),
            P("tile"),
            P("tile", None, None),
            P("tile", None, None),
        ),
        out_specs=(P(None, "tile", None), P(None, "band", "tile"), P("tile")),
        check_vma=False,
    )
```

```python
import functools

import jax
import jax.numpy as jnp
from jax import lax
from jax.experimental import pallas as pl
from jax.experimental.pallas import tpu as pltpu
from jax.sharding import PartitionSpec as P


ITERS = 2
F32 = jnp.float32
BF16 = jnp.bfloat16
HIGH = lax.Precision.HIGHEST
KPAD = 16
ROWS = 10
GROUP = 6
SMALL = 8 << 20
EXTRA = 8
NN = (((1,), (0,)), ((), ()))
NT = (((1,), (1,)), ((), ()))
TN = (((0,), (0,)), ((), ()))


def halves(x):
    hi = x.astype(BF16)
    return hi, (x - hi.astype(F32)).astype(BF16)


def pick(onehot, x, dims=NN):
    n = x.shape[1]
    both = jnp.concatenate(halves(x), axis=1)
    y = lax.dot_general(onehot, both, dims, preferred_element_type=F32)
    return y[:, :n] + y[:, n:]


def exact(a, b, dims):
    return lax.dot_general(a, b, dims, precision=HIGH, preferred_element_type=F32)


def iota(shape, dim):
    return lax.broadcasted_iota(jnp.int32, shape, dim)


def hot(mask):
    return jnp.where(mask, 1.0, 0.0).astype(BF16)


def slot_row(idx):
    cap, peers = idx.shape
    slots = cap * peers
    spread = hot(iota((peers, slots), 1) % peers == iota((peers, slots), 0))
    hi, lo = halves(idx.astype(F32))
    wide = jnp.dot(hi, spread, preferred_element_type=F32) + jnp.dot(
        lo, spread, preferred_element_type=F32
    )
    own = iota((cap, slots), 1) // peers == iota((cap, slots), 0)
    return jnp.sum(jnp.where(own, wide, 0.0), axis=0, keepdims=True)


def slot_column(idx):
    row = slot_row(idx)
    n = row.shape[1]
    return jnp.sum(jnp.where(iota((n, n), 0) == iota((n, n), 1), row, 0.0), axis=1, keepdims=True)


def slots_by_block(idx, blocks):
    slots = idx.shape[0] * idx.shape[1]
    return hot(slot_column(idx) == iota((slots, blocks), 1).astype(F32))


def blocks_by_slot(idx, blocks):
    slots = idx.shape[0] * idx.shape[1]
    return hot(slot_row(idx) == iota((blocks, slots), 0).astype(F32))


def membership_of(lengths, blocks, first=0):
    n = lengths.shape[1]
    upto = hot(iota((n, n), 0) <= iota((n, n), 1))
    rows = jnp.broadcast_to(lengths.astype(F32), (8, n))
    ends = lax.dot_general(rows.astype(BF16), upto, NN, preferred_element_type=F32)[:1]
    starts = ends - lengths.astype(F32)
    position = (iota((blocks, n), 0) + first).astype(F32)
    return hot((position >= starts) & (position < ends))


def band_place():
    me = lax.axis_index("band")
    return me // 2, me % 2


def write_message(out, leaving, colours):
    peers = out.shape[0] // ROWS
    lane = iota((peers, 128), 1)
    for k2 in range(2):
        for j in range(4):
            out[pl.ds(k2 * 4 + j, peers, stride=ROWS), :] = leaving[k2][j * peers : (j + 1) * peers]
    for jj in range(2):
        low = colours[jj * peers : (jj + 1) * peers]
        high = colours[(jj + 2) * peers : (jj + 3) * peers]
        out[pl.ds(8 + jj, peers, stride=ROWS), :] = jnp.where(lane < 64, low, high)


def colour_table(member, colour):
    twice = jnp.concatenate([colour, colour], axis=0)
    hi, lo = halves(twice)
    mid = lax.dot_general(member, hi, NT, preferred_element_type=F32)
    return mid + lax.dot_general(member, lo, NT, preferred_element_type=F32)


def started(copies):
    for c in copies:
        c.start()
    return copies


def begin(spectra, lengths, counts, colour, blocks):
    _, h = band_place()
    channels, _, blends = spectra.shape
    member = membership_of(lengths[...], blocks)
    rel = iota((8, blends), 0)
    absolute = jnp.where(rel < 4, rel ^ (2 * h), 8)
    live = jnp.where(absolute < counts[...], 1.0, 0.0).astype(F32)
    colour[...] = jnp.zeros(colour.shape, F32)
    for c in range(channels):
        for k in range(4):
            colour[pl.ds(k * KPAD + c, 1), :] = spectra[c, pl.ds(k ^ (2 * h), 1), :]
    for k in range(4):
        at = pl.ds(k * KPAD, KPAD)
        colour[at, :] = colour[at, :] * live[k : k + 1]
    wide = jnp.concatenate([live, jnp.zeros((120, blends), F32)], axis=0).astype(BF16)
    ab = lax.dot_general(member, wide, NT, preferred_element_type=F32)
    return live, ab, colour_table(member, colour[...])


def first_kernel(
    morph_far,
    spectra_far,
    lengths_far,
    counts_far,
    sent_far,
    message_far,
    morph,
    spectra,
    lengths,
    counts,
    sent,
    colour,
    message,
    sems,
):
    _, h = band_place()
    near = (lengths, counts, spectra, sent, morph)
    far = (lengths_far, counts_far, spectra_far, sent_far, morph_far.at[pl.ds(2 * h, 2)])
    arrivals = started(
        [pltpu.make_async_copy(f, n, sems.at[i]) for i, (f, n) in enumerate(zip(far, near))]
    )
    blocks = morph.shape[1]
    for c in arrivals[:3]:
        c.wait()
    _, ab, table = begin(spectra, lengths, counts, colour, blocks)
    for c in arrivals[3:]:
        c.wait()
    take = slots_by_block(sent[0], blocks)
    leaving = [pick(take, morph[k2] * ab[:, k2 : k2 + 1]) for k2 in range(2)]
    write_message(message, leaving, pick(take, table))
    pltpu.sync_copy(message, message_far)


def start_kernel(
    morph, spectra, lengths, counts, sent, land, own, other, colour, alive, table, ablk, *kept
):
    _, h = band_place()
    live, ab, rows = begin(spectra, lengths, counts, colour, own.shape[1])
    alive[...] = live
    ablk[...] = ab
    table[...] = rows
    for k2 in range(2):
        own[k2] = morph[k2 ^ (2 * h)] * ab[:, k2 : k2 + 1]
        other[k2] = morph[(k2 + 2) ^ (2 * h)] * ab[:, k2 + 2 : k2 + 3]
    for copy, value in zip(kept, (lengths, sent, land)):
        copy[...] = value[...]


def model_kernel(table, own, other, observed_far, out_far, observed, out, sem_in, sem_out):
    channels, blocks, _ = observed.shape

    def there(t):
        return slice(None), pl.ds(pl.multiple_of(t * 128, 128), 128)

    def arrival(t):
        return pltpu.make_async_copy(observed_far.at[there(t)], observed.at[there(t)], sem_in.at[t])

    def leaving(t):
        return pltpu.make_async_copy(out.at[there(t)], out_far.at[there(t)], sem_out.at[t])

    for t in range(blocks // 128):
        arrival(t).start()

    def tile(t, carry):
        arrival(t).wait()
        rows = pl.ds(pl.multiple_of(t * 128, 128), 128)
        cb = table[rows, :]
        sh = [own[0, rows, :], own[1, rows, :], other[0, rows, :], other[1, rows, :]]
        for c in range(channels):
            m = sh[0] * cb[:, c : c + 1]
            for k in range(1, 4):
                m = m + sh[k] * cb[:, k * KPAD + c : k * KPAD + c + 1]
            out[c, rows, :] = m - observed[c, rows, :]
        leaving(t).start()
        return carry

    lax.fori_loop(0, blocks // 128, tile, 0)
    for t in range(blocks // 128):
        leaving(t).wait()


def link_kernel(
    last,
    mine,
    partner,
    resid_far,
    weights_far,
    land,
    wout_far,
    keep,
    send,
    miss,
    shs,
    back,
    sbs,
    ssb,
    macc,
    resid,
    weights,
    wout,
    sem_r,
    sem_w,
    sem_out,
):
    channels, blocks, pixels = resid.shape
    peers = land.shape[2]
    slots = 4 * peers

    def arrivals(c):
        return (
            pltpu.make_async_copy(resid_far.at[c], resid.at[c], sem_r.at[c]),
            pltpu.make_async_copy(weights_far.at[c], weights.at[c], sem_w.at[c]),
        )

    def gone(c):
        return pltpu.make_async_copy(wout.at[c], wout_far.at[c], sem_out.at[c])

    for c in range(GROUP):
        started(arrivals(c))
    sbs[...] = blocks_by_slot(land[0], blocks)
    ssb[...] = slots_by_block(land[0], blocks)
    for k2 in range(2):
        for j in range(4):
            rows = pl.ds(j * peers, peers)
            shs[k2, rows, :] = mine[pl.ds(k2 * 4 + j, peers, stride=ROWS), :]
            shs[k2 + 2, rows, :] = partner[pl.ds(k2 * 4 + j, peers, stride=ROWS), :]
    back[...] = jnp.zeros(back.shape, F32)
    if last:
        macc[...] = jnp.zeros(macc.shape, F32)
    lane = iota((peers, 128), 1)

    def group(g, carry):
        ci, bc = carry[:2], list(carry[2:])

        @pl.when(g + 1 < channels // GROUP)
        def _():
            for u in range(GROUP):
                started(arrivals((g + 1) * GROUP + u))

        for u in range(GROUP):
            for a in arrivals(g * GROUP + u):
                a.wait()
        for u in range(GROUP):
            c = g * GROUP + u
            parts = []
            for j in range(4):
                rows = pl.ds(j * peers, peers)
                at = u + (64 if j >= 2 else 0)
                m = shs[0, rows, :] * ci[j % 2][:, at : at + 1]
                for k in range(1, 4):
                    col = at + k * KPAD
                    m = m + shs[k, rows, :] * ci[j % 2][:, col : col + 1]
                parts.append(m)
            both = jnp.concatenate(halves(jnp.concatenate(parts, axis=0)), axis=1)
            landed = jnp.zeros((slots, 2 * pixels), F32)
            for q in range(blocks // 128):
                rows = pl.ds(q * 128, 128)
                y = jnp.dot(sbs[rows, :], both, preferred_element_type=F32)
                x = resid[c, rows, :] + (y[:, :pixels] + y[:, pixels:])
                wt = weights[c, rows, :] * x
                wout[c, rows, :] = wt
                if last:
                    macc[rows, :] += wt * x
                wboth = jnp.concatenate(halves(wt), axis=1)
                landed = landed + jnp.dot(ssb[:, rows], wboth, preferred_element_type=F32)
            landed = landed[:, :pixels] + landed[:, pixels:]
            for j in range(4):
                rows = pl.ds(j * peers, peers)
                at = u + (64 if j >= 2 else 0)
                ld = landed[j * peers : (j + 1) * peers]
                for k in range(4):
                    col = at + k * KPAD
                    back[k, rows, :] += ci[j % 2][:, col : col + 1] * ld
                    r = jnp.sum(shs[k, rows, :] * ld, axis=1, keepdims=True)
                    bc[j % 2] = jnp.where(lane == col, r, bc[j % 2])
        for u in range(GROUP):
            gone(g * GROUP + u).start()
        return tuple(pltpu.roll(v, 128 - GROUP, 1) for v in (*ci, *bc))

    ci = tuple(mine[pl.ds(8 + jj, peers, stride=ROWS), :] for jj in range(2))
    none = jnp.zeros((peers, 128), F32)
    done = lax.fori_loop(0, channels // GROUP, group, (*ci, none, none))
    bc = [pltpu.roll(v, channels, 1) for v in done[2:]]
    keep[...] = jnp.zeros(keep.shape, F32)
    send[...] = jnp.zeros(send.shape, F32)
    for k2 in range(2):
        for j in range(4):
            rows = pl.ds(j * peers, peers)
            keep[pl.ds(k2 * 4 + j, peers, stride=ROWS), :] = back[k2, rows, :]
            send[pl.ds(k2 * 4 + j, peers, stride=ROWS), :] = back[k2 + 2, rows, :]
    for jj in range(2):
        keep[pl.ds(8 + jj, peers, stride=ROWS), :] = bc[jj]
    if last:
        miss[...] = exact(jnp.ones((8, pixels), F32), macc[...], NT)
    else:
        miss[...] = jnp.zeros(miss.shape, F32)
    for c in range(channels):
        gone(c).wait()


def grad_kernel(
    table, own, other, wgt_far, colour, lengths, miss, after, keep, send, per_block, wgt, sems
):
    channels, blocks, _ = wgt.shape

    def arrival(t):
        there = slice(None), pl.ds(pl.multiple_of(t * 128, 128), 128)
        return pltpu.make_async_copy(wgt_far.at[there], wgt.at[there], sems.at[t])

    for t in range(blocks // 128):
        arrival(t).start()
    lane = iota((128, 128), 1)
    quarter = blocks // 4

    def colours(t, carry):
        arrival(t).wait()
        rows = pl.ds(pl.multiple_of(t * 128, 128), 128)
        sh = [own[0, rows, :], own[1, rows, :], other[0, rows, :], other[1, rows, :]]
        pb = jnp.zeros((128, 128), F32)
        for c in range(channels):
            wt = wgt[c, rows, :]
            for k in range(4):
                r = jnp.sum(sh[k] * wt, axis=1, keepdims=True)
                pb = jnp.where(lane == k * KPAD + c, r, pb)
        per_block[rows, :] = pb
        return carry

    lax.fori_loop(0, blocks // 128, colours, 0)

    def shapes(t, carry):
        q, inside = t // 2, pl.multiple_of((t % 2) * 64, 64)
        rows = pl.ds(pl.multiple_of(t * 64, 64), 64)
        cb = table[rows, :]
        gs = [None] * 4
        for c in range(channels):
            wt = wgt[c, rows, :]
            for k in range(4):
                term = cb[:, k * KPAD + c : k * KPAD + c + 1] * wt
                gs[k] = term if c == 0 else gs[k] + term
        for k2 in range(2):
            keep[q, pl.ds(k2 * quarter + inside, 64), :] = gs[k2]
            send[q, pl.ds(k2 * quarter + inside, 64), :] = gs[k2 + 2]
        return carry

    lax.fori_loop(0, blocks // 64, shapes, 0)
    member = membership_of(lengths[...], blocks)
    sq = colour[...] * colour[...]
    rows8 = iota((8, sq.shape[1]), 0)
    power = jnp.zeros((8, sq.shape[1]), F32)
    for k in range(4):
        total = jnp.sum(sq[k * KPAD : (k + 1) * KPAD], axis=0, keepdims=True)
        power = jnp.where(rows8 == k, total, power)
    hi, lo = halves(power)
    wide = lax.dot_general(hi, member, NT, preferred_element_type=F32) + lax.dot_general(
        lo, member, NT, preferred_element_type=F32
    )
    for q in range(4):
        w = wide[:, q * quarter : (q + 1) * quarter]
        m = miss[0:1, q * quarter : (q + 1) * quarter]
        r = iota((8, quarter), 0)
        first = jnp.where(r == 0, m, jnp.where(r == 1, w[0:1], jnp.where(r == 2, w[1:2], 0.0)))
        second = jnp.where(r == 0, m, jnp.where(r == 1, w[2:3], jnp.where(r == 2, w[3:4], 0.0)))
        keep[q, pl.ds(2 * quarter, EXTRA), :] = first
        send[q, pl.ds(2 * quarter, EXTRA), :] = second


def merge_kernel(arrived, keep, came, sent, p0, p1, p2, p3, scat):
    x, _ = band_place()
    peers = sent.shape[2]
    quarter = (p0.shape[0] - EXTRA) // 2
    blocks = 4 * quarter
    put = blocks_by_slot(sent[0], blocks)
    for k2 in range(2):
        rows = [arrived[pl.ds(k2 * 4 + j, peers, stride=ROWS), :] for j in range(4)]
        scat[k2] = pick(put, jnp.concatenate(rows, axis=0))
    for step, out in enumerate((p0, p1, p2, p3)):
        q = lax.rem(x + step, 4)
        out[...] = keep[q] + came[q]
        for k2 in range(2):
            at = pl.ds(pl.multiple_of(q * quarter, quarter), quarter)
            out[pl.ds(k2 * quarter, quarter), :] += scat[k2, at, :]


def colour_kernel(
    last, arrived, sent, per_block, lengths, own, other, colour, alive, *outs
):
    if last:
        out, fresh = outs
    else:
        fresh, table = outs
    blocks = per_block.shape[0]
    peers = sent.shape[2]
    member = membership_of(lengths[...], blocks)
    put = blocks_by_slot(sent[0], blocks)
    lane = iota((peers, 128), 1)
    rows = []
    for j in range(4):
        row = arrived[pl.ds(8 + j % 2, peers, stride=ROWS), :]
        rows.append(jnp.where((lane < 64) == (j < 2), row, 0.0))
    total = per_block[...] + pick(put, jnp.concatenate(rows, axis=0))
    hi, lo = halves(total)
    grad = lax.dot_general(hi, member, TN, preferred_element_type=F32) + lax.dot_general(
        lo, member, TN, preferred_element_type=F32
    )
    grad = grad[:64] + grad[64:]
    ones = jnp.ones((8, own.shape[2]), F32)
    for k in range(4):
        s = own[k] if k < 2 else other[k - 2]
        by_block = exact(ones, s * s, NT)
        hi, lo = halves(by_block)
        power = lax.dot_general(hi, member, NN, preferred_element_type=F32) + lax.dot_general(
            lo, member, NN, preferred_element_type=F32
        )
        step = 1.0 / (1.0 + power[:1])
        at = pl.ds(k * KPAD, KPAD)
        new = (
            jnp.maximum(colour[at, :] - step * grad[k * KPAD : (k + 1) * KPAD], 0.0)
            * alive[k : k + 1, :]
        )
        fresh[at, :] = new
    if last:
        _, h = band_place()
        for c in range(out.shape[0]):
            for k in range(4):
                out[c, pl.ds(k ^ (2 * h), 1), :] = fresh[pl.ds(k * KPAD + c, 1), :]
    else:
        table[...] = colour_table(member, fresh[...])


def update_kernel(p0, r1, r2, r3, own, ablk, out):
    x, _ = band_place()
    quarter = (p0.shape[0] - EXTRA) // 2
    total = p0[...] + r1[...] + r2[...] + r3[...]
    at = pl.ds(pl.multiple_of(x * quarter, quarter), quarter)
    ab = ablk[at, :]
    eye = iota((quarter, quarter), 0) == iota((quarter, quarter), 1)
    for k2 in range(2):
        row = total[2 * quarter + 1 + k2 : 2 * quarter + 2 + k2]
        power = jnp.sum(jnp.where(eye, row, 0.0), axis=1, keepdims=True)
        step = 1.0 / (1.0 + power)
        g = total[k2 * quarter : (k2 + 1) * quarter]
        out[pl.ds(k2 * quarter, quarter), :] = (
            jnp.maximum(own[k2, at, :] - step * g, 0.0) * ab[:, k2 : k2 + 1]
        )
    out[pl.ds(2 * quarter, EXTRA), :] = total[2 * quarter :]


def leave_kernel(n0, r1, r2, r3, table, sent, pair, message_far, message):
    x, _ = band_place()
    quarter = (n0.shape[0] - EXTRA) // 2
    for step, piece in enumerate((n0, r1, r2, r3)):
        q = lax.rem(x + 4 - step, 4)
        at = pl.ds(pl.multiple_of(q * quarter, quarter), quarter)
        for k2 in range(2):
            pair[k2, at, :] = piece[pl.ds(k2 * quarter, quarter), :]
    take = slots_by_block(sent[0], 4 * quarter)
    write_message(message, [pick(take, pair[0]), pick(take, pair[1])], pick(take, table[...]))
    pltpu.sync_copy(message, message_far)


def finish_kernel(n0, r1, r2, r3, m0, m1, m2, m3, lengths, shape, misfit):
    x, h = band_place()
    quarter = (n0.shape[0] - EXTRA) // 2
    total = jnp.zeros((8, lengths.shape[1]), F32)
    for step, (mine, theirs) in enumerate(((n0, m0), (r1, m1), (r2, m2), (r3, m3))):
        q = lax.rem(x + 4 - step, 4)
        at = pl.ds(pl.multiple_of(q * quarter, quarter), quarter)
        for k2 in range(2):
            shape[k2 + 2 * h, at, :] = mine[pl.ds(k2 * quarter, quarter), :]
            shape[k2 + 2 * (1 - h), at, :] = theirs[pl.ds(k2 * quarter, quarter), :]
        ms = mine[pl.ds(2 * quarter, EXTRA), :]
        part = membership_of(lengths[...], quarter, q * quarter)
        hi, lo = halves(ms)
        total = total + lax.dot_general(hi, part, NN, preferred_element_type=F32)
        total = total + lax.dot_general(lo, part, NN, preferred_element_type=F32)
    misfit[...] = total[:1]


def call(kernel, outs, args, scratch=(), limit=54_000_000, cost=3e6, far_in=(), far_out=()):
    many = isinstance(outs, list)
    shapes = [
        s if isinstance(s, jax.ShapeDtypeStruct) else jax.ShapeDtypeStruct(s, F32)
        for s in (outs if many else [outs])
    ]
    near = pl.BlockSpec(memory_space=pltpu.VMEM)
    far = pl.BlockSpec(memory_space=pltpu.HBM)
    got = pl.pallas_call(
        kernel,
        out_shape=shapes,
        in_specs=[far if i in far_in else near for i in range(len(args))],
        out_specs=[far if i in far_out else near for i in range(len(shapes))],
        scratch_shapes=list(scratch),
        compiler_params=pltpu.CompilerParams(vmem_limit_bytes=limit),
        cost_estimate=pl.CostEstimate(flops=0, bytes_accessed=int(cost), transcendentals=0),
    )(*args)
    return got if many else got[0]


def on_device(
    observed, weights, morphology, spectra, blend_blocks, source_count, sent_blocks, landing_blocks
):
    channels, blocks, pixels = observed.shape
    spectra = spectra.transpose(1, 0, 2)
    sent_blocks = sent_blocks.transpose(0, 2, 1)
    landing_blocks = landing_blocks.transpose(0, 2, 1)
    blends = spectra.shape[2]
    peers = sent_blocks.shape[2]
    slots = 4 * peers
    quarter = blocks // 4
    piece = (2 * quarter + EXTRA, pixels)
    pair = (2, blocks, pixels)
    message = (peers * ROWS, pixels)
    band = lax.axis_size("band")

    def over_core(v):
        return lax.ppermute(v, "band", [(i, i ^ 1) for i in range(band)])

    def over_x(v, step):
        return lax.ppermute(v, "band", [(i, (i + 2 * step) % band) for i in range(band)])

    def over_tile(v):
        v = v.reshape(peers, ROWS // 2, 2, pixels)
        return lax.all_to_all(v, "tile", 0, 0, tiled=True).reshape(message)

    counts = source_count.reshape(1, blends)
    colour_rows = (4 * KPAD, blends)
    table_rows = (blocks, 128)

    def kept(v):
        return jax.ShapeDtypeStruct(v.shape, v.dtype)

    def dma(n):
        return pltpu.SemaphoreType.DMA((n,))

    cube = pltpu.VMEM(observed.shape, F32)
    leaving = call(
        first_kernel,
        message,
        (morphology, spectra, blend_blocks, counts, sent_blocks),
        scratch=(
            pltpu.VMEM(pair, F32),
            pltpu.VMEM(spectra.shape, F32),
            pltpu.VMEM(blend_blocks.shape, jnp.int32),
            pltpu.VMEM(counts.shape, jnp.int32),
            pltpu.VMEM(sent_blocks.shape, jnp.int32),
            pltpu.VMEM(colour_rows, F32),
            pltpu.VMEM(message, F32),
            dma(5),
        ),
        limit=67_043_328,
        far_in=range(5),
        far_out=(0,),
    )
    own, other, colour, alive, table, ablk, lengths, sent, land = call(
        start_kernel,
        [
            pair,
            pair,
            colour_rows,
            (8, blends),
            table_rows,
            table_rows,
            kept(blend_blocks),
            kept(sent_blocks),
            kept(landing_blocks),
        ],
        (morphology, spectra, blend_blocks, counts, sent_blocks, landing_blocks),
    )
    for iteration in range(ITERS):
        last = iteration == ITERS - 1
        mine = over_tile(leaving)
        resid = call(
            model_kernel,
            observed.shape,
            (table, own, other, observed),
            scratch=(cube, cube, dma(blocks // 128), dma(blocks // 128)),
            cost=16e6,
            far_in=(3,),
            far_out=(0,),
        )
        mine, resid = lax.optimization_barrier((mine, resid))
        partner = over_core(mine)
        wgt, bkeep, bsend, miss = call(
            functools.partial(link_kernel, last),
            [observed.shape, message, message, (8, blocks)],
            (mine, partner, resid, weights, land),
            scratch=(
                pltpu.VMEM((4, slots, pixels), F32),
                pltpu.VMEM((4, slots, pixels), F32),
                pltpu.VMEM((blocks, slots), BF16),
                pltpu.VMEM((slots, blocks), BF16),
                pltpu.VMEM((blocks, pixels), F32),
                cube,
                cube,
                cube,
                dma(channels),
                dma(channels),
                dma(channels),
            ),
            cost=14e6,
            far_in=(2, 3),
            far_out=(0,),
        )
        returning = bkeep + over_core(bsend)
        back = over_tile(returning)
        gkeep, gsend, per_block = call(
            grad_kernel,
            [(4,) + piece, (4,) + piece, table_rows],
            (table, own, other, wgt, colour, lengths, miss, returning),
            scratch=(cube, dma(blocks // 128)),
            cost=30e6,
            far_in=(3, 7),
        )
        gcame = over_core(gsend)
        p0, p1, p2, p3 = call(
            merge_kernel,
            [piece] * 4,
            (back, gkeep, gcame, sent),
            scratch=(pltpu.VMEM(pair, F32),),
            limit=SMALL,
        )
        r1, r2, r3 = (over_x(v, s) for s, v in ((1, p1), (2, p2), (3, p3)))
        colour_args = (back, sent, per_block, lengths, own, other, colour, alive)
        if last:
            new_colour = call(
                functools.partial(colour_kernel, True),
                (channels, 4, blends),
                colour_args,
                scratch=(pltpu.VMEM(colour_rows, F32),),
                limit=SMALL,
                cost=8e6,
            )
        else:
            colour, table = call(
                functools.partial(colour_kernel, False),
                [colour_rows, table_rows],
                colour_args,
                limit=SMALL,
                cost=8e6,
            )
        n0 = call(update_kernel, piece, (p0, r1, r2, r3, own, ablk), limit=SMALL)
        n1, n2, n3 = (over_x(n0, s) for s in (1, 2, 3))
        if not last:
            own, leaving = call(
                leave_kernel, [pair, message], (n0, n1, n2, n3, table, sent),
                scratch=(pltpu.VMEM(message, F32),),
                limit=SMALL,
                far_out=(1,),
            )
            other = over_core(own)
    m0, m1, m2, m3 = (over_core(v) for v in (n0, n1, n2, n3))
    shape, misfit = call(
        finish_kernel,
        [morphology.shape, (1, blends)],
        (n0, n1, n2, n3, m0, m1, m2, m3, lengths),
        limit=SMALL,
    )
    return shape, new_colour.transpose(1, 0, 2), misfit.reshape(blends)


def solution(mesh):
    return jax.shard_map(
        on_device,
        mesh=mesh,
        in_specs=(
            P("band", "tile", None),
            P("band", "tile", None),
            P(None, "tile", None),
            P(None, "band", "tile"),
            P("tile", None),
            P("tile"),
            P("tile", None, None),
            P("tile", None, None),
        ),
        out_specs=(P(None, "tile", None), P(None, "band", "tile"), P("tile")),
        check_vma=False,
    )
```

```python
import functools

import jax
import jax.numpy as jnp
from jax import lax
from jax.experimental import pallas as pl
from jax.experimental.pallas import tpu as pltpu
from jax.sharding import PartitionSpec as P


ITERS = 2
F32 = jnp.float32
BF16 = jnp.bfloat16
HIGH = lax.Precision.HIGHEST
KPAD = 16
ROWS = 10
GROUP = 6
SMALL = 8 << 20
EXTRA = 8
NN = (((1,), (0,)), ((), ()))
NT = (((1,), (1,)), ((), ()))
TN = (((0,), (0,)), ((), ()))


def halves(x):
    hi = x.astype(BF16)
    return hi, (x - hi.astype(F32)).astype(BF16)


def pick(onehot, x, dims=NN):
    n = x.shape[1]
    both = jnp.concatenate(halves(x), axis=1)
    y = lax.dot_general(onehot, both, dims, preferred_element_type=F32)
    return y[:, :n] + y[:, n:]


def exact(a, b, dims):
    return lax.dot_general(a, b, dims, precision=HIGH, preferred_element_type=F32)


def iota(shape, dim):
    return lax.broadcasted_iota(jnp.int32, shape, dim)


def hot(mask):
    return jnp.where(mask, 1.0, 0.0).astype(BF16)


def slot_row(idx):
    cap, peers = idx.shape
    slots = cap * peers
    spread = hot(iota((peers, slots), 1) % peers == iota((peers, slots), 0))
    hi, lo = halves(idx.astype(F32))
    wide = jnp.dot(hi, spread, preferred_element_type=F32) + jnp.dot(
        lo, spread, preferred_element_type=F32
    )
    own = iota((cap, slots), 1) // peers == iota((cap, slots), 0)
    return jnp.sum(jnp.where(own, wide, 0.0), axis=0, keepdims=True)


def slot_column(idx):
    row = slot_row(idx)
    n = row.shape[1]
    return jnp.sum(jnp.where(iota((n, n), 0) == iota((n, n), 1), row, 0.0), axis=1, keepdims=True)


def slots_by_block(idx, blocks):
    slots = idx.shape[0] * idx.shape[1]
    return hot(slot_column(idx) == iota((slots, blocks), 1).astype(F32))


def blocks_by_slot(idx, blocks):
    slots = idx.shape[0] * idx.shape[1]
    return hot(slot_row(idx) == iota((blocks, slots), 0).astype(F32))


def membership_of(lengths, blocks, first=0):
    n = lengths.shape[1]
    upto = hot(iota((n, n), 0) <= iota((n, n), 1))
    rows = jnp.broadcast_to(lengths.astype(F32), (8, n))
    ends = lax.dot_general(rows.astype(BF16), upto, NN, preferred_element_type=F32)[:1]
    starts = ends - lengths.astype(F32)
    position = (iota((blocks, n), 0) + first).astype(F32)
    return hot((position >= starts) & (position < ends))


def band_place():
    me = lax.axis_index("band")
    return me // 2, me % 2


def write_message(out, leaving, colours):
    peers = out.shape[0] // ROWS
    lane = iota((peers, 128), 1)
    for k2 in range(2):
        for j in range(4):
            out[pl.ds(k2 * 4 + j, peers, stride=ROWS), :] = leaving[k2][j * peers : (j + 1) * peers]
    for jj in range(2):
        low = colours[jj * peers : (jj + 1) * peers]
        high = colours[(jj + 2) * peers : (jj + 3) * peers]
        out[pl.ds(8 + jj, peers, stride=ROWS), :] = jnp.where(lane < 64, low, high)


def colour_table(member, colour):
    twice = jnp.concatenate([colour, colour], axis=0)
    hi, lo = halves(twice)
    mid = lax.dot_general(member, hi, NT, preferred_element_type=F32)
    return mid + lax.dot_general(member, lo, NT, preferred_element_type=F32)


def started(copies):
    for c in copies:
        c.start()
    return copies


def begin(spectra, lengths, counts, colour, blocks):
    _, h = band_place()
    channels, _, blends = spectra.shape
    member = membership_of(lengths[...], blocks)
    rel = iota((8, blends), 0)
    absolute = jnp.where(rel < 4, rel ^ (2 * h), 8)
    live = jnp.where(absolute < counts[...], 1.0, 0.0).astype(F32)
    colour[...] = jnp.zeros(colour.shape, F32)
    for c in range(channels):
        for k in range(4):
            colour[pl.ds(k * KPAD + c, 1), :] = spectra[c, pl.ds(k ^ (2 * h), 1), :]
    for k in range(4):
        at = pl.ds(k * KPAD, KPAD)
        colour[at, :] = colour[at, :] * live[k : k + 1]
    wide = jnp.concatenate([live, jnp.zeros((120, blends), F32)], axis=0).astype(BF16)
    ab = lax.dot_general(member, wide, NT, preferred_element_type=F32)
    return live, ab, colour_table(member, colour[...])


def first_kernel(
    morph_far,
    spectra_far,
    lengths_far,
    counts_far,
    sent_far,
    message_far,
    morph,
    spectra,
    lengths,
    counts,
    sent,
    colour,
    message,
    sems,
):
    _, h = band_place()
    near = (lengths, counts, spectra, sent, morph)
    far = (lengths_far, counts_far, spectra_far, sent_far, morph_far.at[pl.ds(2 * h, 2)])
    arrivals = started(
        [pltpu.make_async_copy(f, n, sems.at[i]) for i, (f, n) in enumerate(zip(far, near))]
    )
    blocks = morph.shape[1]
    for c in arrivals[:3]:
        c.wait()
    _, ab, table = begin(spectra, lengths, counts, colour, blocks)
    for c in arrivals[3:]:
        c.wait()
    take = slots_by_block(sent[0], blocks)
    leaving = [pick(take, morph[k2] * ab[:, k2 : k2 + 1]) for k2 in range(2)]
    write_message(message, leaving, pick(take, table))
    pltpu.sync_copy(message, message_far)


def powers(colour, member):
    sq = colour * colour
    rows8 = iota((8, sq.shape[1]), 0)
    power = jnp.zeros((8, sq.shape[1]), F32)
    for k in range(4):
        total = jnp.sum(sq[k * KPAD : (k + 1) * KPAD], axis=0, keepdims=True)
        power = jnp.where(rows8 == k, total, power)
    hi, lo = halves(power)
    return lax.dot_general(hi, member, NT, preferred_element_type=F32) + lax.dot_general(
        lo, member, NT, preferred_element_type=F32
    )


def tile_copies(far, near, sems, out=False):
    def copy(t):
        there = slice(None), pl.ds(pl.multiple_of(t * 128, 128), 128)
        ends = (near.at[there], far.at[there]) if out else (far.at[there], near.at[there])
        return pltpu.make_async_copy(*ends, sems.at[t])

    return copy


def model_loop(table, own, other, observed, out, arrival, leaving):
    channels, blocks, _ = observed.shape

    def tile(t, carry):
        arrival(t).wait()
        rows = pl.ds(pl.multiple_of(t * 128, 128), 128)
        cb = table[rows, :]
        sh = [own[0, rows, :], own[1, rows, :], other[0, rows, :], other[1, rows, :]]
        for c in range(channels):
            m = sh[0] * cb[:, c : c + 1]
            for k in range(1, 4):
                m = m + sh[k] * cb[:, k * KPAD + c : k * KPAD + c + 1]
            out[c, rows, :] = m - observed[c, rows, :]
        leaving(t).start()
        return carry

    lax.fori_loop(0, blocks // 128, tile, 0)


def start_kernel(
    morph_far,
    spectra_far,
    lengths_far,
    counts_far,
    sent_far,
    land_far,
    observed_far,
    own,
    other,
    colour,
    alive,
    table,
    ablk,
    lengths,
    sent,
    land,
    wide,
    resid_far,
    morph,
    spectra,
    counts,
    observed,
    resid,
    sems,
    sem_in,
    sem_out,
):
    _, h = band_place()
    near = (lengths, counts, spectra, sent, land, morph)
    far = (lengths_far, counts_far, spectra_far, sent_far, land_far, morph_far)
    arrivals = started(
        [pltpu.make_async_copy(f, n, sems.at[i]) for i, (f, n) in enumerate(zip(far, near))]
    )
    arrival = tile_copies(observed_far, observed, sem_in)
    leaving = tile_copies(resid_far, resid, sem_out, out=True)
    blocks = own.shape[1]
    tiles = range(blocks // 128)
    started([arrival(t) for t in tiles])
    for c in arrivals[:3]:
        c.wait()
    live, ab, rows = begin(spectra, lengths, counts, colour, blocks)
    alive[...] = live
    ablk[...] = ab
    table[...] = rows
    for c in arrivals[3:]:
        c.wait()
    for k2 in range(2):
        own[k2] = morph[k2 ^ (2 * h)] * ab[:, k2 : k2 + 1]
        other[k2] = morph[(k2 + 2) ^ (2 * h)] * ab[:, k2 + 2 : k2 + 3]
    model_loop(table, own, other, observed, resid, arrival, leaving)
    wide[...] = powers(colour[...], membership_of(lengths[...], blocks))
    for t in tiles:
        leaving(t).wait()


def model_kernel(
    table,
    own,
    other,
    colour,
    lengths,
    observed_far,
    wide,
    resid_far,
    observed,
    resid,
    sem_in,
    sem_out,
):
    arrival = tile_copies(observed_far, observed, sem_in)
    leaving = tile_copies(resid_far, resid, sem_out, out=True)
    blocks = own.shape[1]
    tiles = range(blocks // 128)
    started([arrival(t) for t in tiles])
    wide[...] = powers(colour[...], membership_of(lengths[...], blocks))
    model_loop(table, own, other, observed, resid, arrival, leaving)
    for t in tiles:
        leaving(t).wait()


def link_kernel(
    last,
    mine,
    partner,
    resid_far,
    weights_far,
    land,
    wout_far,
    keep,
    send,
    miss,
    shs,
    back,
    sbs,
    ssb,
    macc,
    resid,
    weights,
    wout,
    sem_r,
    sem_w,
    sem_out,
):
    channels, blocks, pixels = resid.shape
    peers = land.shape[2]
    slots = 4 * peers

    def arrivals(c):
        return (
            pltpu.make_async_copy(resid_far.at[c], resid.at[c], sem_r.at[c]),
            pltpu.make_async_copy(weights_far.at[c], weights.at[c], sem_w.at[c]),
        )

    def gone(c):
        return pltpu.make_async_copy(wout.at[c], wout_far.at[c], sem_out.at[c])

    for c in range(GROUP):
        started(arrivals(c))
    sbs[...] = blocks_by_slot(land[0], blocks)
    ssb[...] = slots_by_block(land[0], blocks)
    for k2 in range(2):
        for j in range(4):
            rows = pl.ds(j * peers, peers)
            shs[k2, rows, :] = mine[pl.ds(k2 * 4 + j, peers, stride=ROWS), :]
            shs[k2 + 2, rows, :] = partner[pl.ds(k2 * 4 + j, peers, stride=ROWS), :]
    back[...] = jnp.zeros(back.shape, F32)
    if last:
        macc[...] = jnp.zeros(macc.shape, F32)
    lane = iota((peers, 128), 1)

    def group(g, carry):
        ci, bc = carry[:2], list(carry[2:])

        @pl.when(g + 1 < channels // GROUP)
        def _():
            for u in range(GROUP):
                started(arrivals((g + 1) * GROUP + u))

        for u in range(GROUP):
            for a in arrivals(g * GROUP + u):
                a.wait()
        for u in range(GROUP):
            c = g * GROUP + u
            parts = []
            for j in range(4):
                rows = pl.ds(j * peers, peers)
                at = u + (64 if j >= 2 else 0)
                m = shs[0, rows, :] * ci[j % 2][:, at : at + 1]
                for k in range(1, 4):
                    col = at + k * KPAD
                    m = m + shs[k, rows, :] * ci[j % 2][:, col : col + 1]
                parts.append(m)
            both = jnp.concatenate(halves(jnp.concatenate(parts, axis=0)), axis=1)
            landed = jnp.zeros((slots, 2 * pixels), F32)
            for q in range(blocks // 128):
                rows = pl.ds(q * 128, 128)
                y = jnp.dot(sbs[rows, :], both, preferred_element_type=F32)
                x = resid[c, rows, :] + (y[:, :pixels] + y[:, pixels:])
                wt = weights[c, rows, :] * x
                wout[c, rows, :] = wt
                if last:
                    macc[rows, :] += wt * x
                wboth = jnp.concatenate(halves(wt), axis=1)
                landed = landed + jnp.dot(ssb[:, rows], wboth, preferred_element_type=F32)
            landed = landed[:, :pixels] + landed[:, pixels:]
            for j in range(4):
                rows = pl.ds(j * peers, peers)
                at = u + (64 if j >= 2 else 0)
                ld = landed[j * peers : (j + 1) * peers]
                for k in range(4):
                    col = at + k * KPAD
                    back[k, rows, :] += ci[j % 2][:, col : col + 1] * ld
                    r = jnp.sum(shs[k, rows, :] * ld, axis=1, keepdims=True)
                    bc[j % 2] = jnp.where(lane == col, r, bc[j % 2])
        for u in range(GROUP):
            gone(g * GROUP + u).start()
        return tuple(pltpu.roll(v, 128 - GROUP, 1) for v in (*ci, *bc))

    ci = tuple(mine[pl.ds(8 + jj, peers, stride=ROWS), :] for jj in range(2))
    none = jnp.zeros((peers, 128), F32)
    done = lax.fori_loop(0, channels // GROUP, group, (*ci, none, none))
    bc = [pltpu.roll(v, channels, 1) for v in done[2:]]
    keep[...] = jnp.zeros(keep.shape, F32)
    send[...] = jnp.zeros(send.shape, F32)
    for k2 in range(2):
        for j in range(4):
            rows = pl.ds(j * peers, peers)
            keep[pl.ds(k2 * 4 + j, peers, stride=ROWS), :] = back[k2, rows, :]
            send[pl.ds(k2 * 4 + j, peers, stride=ROWS), :] = back[k2 + 2, rows, :]
    for jj in range(2):
        keep[pl.ds(8 + jj, peers, stride=ROWS), :] = bc[jj]
    if last:
        miss[...] = exact(jnp.ones((8, pixels), F32), macc[...], NT)
    else:
        miss[...] = jnp.zeros(miss.shape, F32)
    for c in range(channels):
        gone(c).wait()


def grad_kernel(table, wgt_far, wide, miss, after, keep, send, wgt, sems):
    channels, blocks, _ = wgt.shape
    quarter = blocks // 4
    arrival = tile_copies(wgt_far, wgt, sems)
    started([arrival(t) for t in range(4)])
    for q in range(4):
        w = wide[:, q * quarter : (q + 1) * quarter]
        m = miss[0:1, q * quarter : (q + 1) * quarter]
        r = iota((8, quarter), 0)
        first = jnp.where(r == 0, m, jnp.where(r == 1, w[0:1], jnp.where(r == 2, w[1:2], 0.0)))
        second = jnp.where(r == 0, m, jnp.where(r == 1, w[2:3], jnp.where(r == 2, w[3:4], 0.0)))
        keep[q, pl.ds(2 * quarter, EXTRA), :] = first
        send[q, pl.ds(2 * quarter, EXTRA), :] = second

    def shapes(q, carry):
        arrival(q).wait()
        for half in range(2):
            rows = pl.ds(pl.multiple_of(q * quarter + half * 64, 64), 64)
            cb = table[rows, :]
            gs = [None] * 4
            for c in range(channels):
                wt = wgt[c, rows, :]
                for k in range(4):
                    term = cb[:, k * KPAD + c : k * KPAD + c + 1] * wt
                    gs[k] = term if c == 0 else gs[k] + term
            for k2 in range(2):
                keep[q, pl.ds(k2 * quarter + half * 64, 64), :] = gs[k2]
                send[q, pl.ds(k2 * quarter + half * 64, 64), :] = gs[k2 + 2]
        return carry

    lax.fori_loop(0, 4, shapes, 0)


def product_kernel(own, other, wgt_far, per_block, wgt, sems):
    channels, blocks, _ = wgt.shape
    lane = iota((128, 128), 1)
    arrival = tile_copies(wgt_far, wgt, sems)
    started([arrival(t) for t in range(blocks // 128)])

    def tile(t, carry):
        arrival(t).wait()
        rows = pl.ds(pl.multiple_of(t * 128, 128), 128)
        sh = [own[0, rows, :], own[1, rows, :], other[0, rows, :], other[1, rows, :]]
        pb = jnp.zeros((128, 128), F32)
        for c in range(channels):
            wt = wgt[c, rows, :]
            for k in range(4):
                r = jnp.sum(sh[k] * wt, axis=1, keepdims=True)
                pb = jnp.where(lane == k * KPAD + c, r, pb)
        per_block[rows, :] = pb
        return carry

    lax.fori_loop(0, blocks // 128, tile, 0)


def merge_kernel(arrived, keep, came, sent, p0, p1, p2, p3, scat):
    x, _ = band_place()
    peers = sent.shape[2]
    quarter = (p0.shape[0] - EXTRA) // 2
    blocks = 4 * quarter
    put = blocks_by_slot(sent[0], blocks)
    for k2 in range(2):
        rows = [arrived[pl.ds(k2 * 4 + j, peers, stride=ROWS), :] for j in range(4)]
        scat[k2] = pick(put, jnp.concatenate(rows, axis=0))
    for step, out in enumerate((p0, p1, p2, p3)):
        q = lax.rem(x + step, 4)
        out[...] = keep[q] + came[q]
        for k2 in range(2):
            at = pl.ds(pl.multiple_of(q * quarter, quarter), quarter)
            out[pl.ds(k2 * quarter, quarter), :] += scat[k2, at, :]


def colour_kernel(
    last, arrived, sent, per_block, lengths, own, other, colour, alive, *outs
):
    if last:
        out, fresh = outs
    else:
        fresh, table = outs
    blocks = per_block.shape[0]
    peers = sent.shape[2]
    member = membership_of(lengths[...], blocks)
    put = blocks_by_slot(sent[0], blocks)
    lane = iota((peers, 128), 1)
    rows = []
    for j in range(4):
        row = arrived[pl.ds(8 + j % 2, peers, stride=ROWS), :]
        rows.append(jnp.where((lane < 64) == (j < 2), row, 0.0))
    total = per_block[...] + pick(put, jnp.concatenate(rows, axis=0))
    hi, lo = halves(total)
    grad = lax.dot_general(hi, member, TN, preferred_element_type=F32) + lax.dot_general(
        lo, member, TN, preferred_element_type=F32
    )
    grad = grad[:64] + grad[64:]
    ones = jnp.ones((8, own.shape[2]), F32)
    for k in range(4):
        s = own[k] if k < 2 else other[k - 2]
        by_block = exact(ones, s * s, NT)
        hi, lo = halves(by_block)
        power = lax.dot_general(hi, member, NN, preferred_element_type=F32) + lax.dot_general(
            lo, member, NN, preferred_element_type=F32
        )
        step = 1.0 / (1.0 + power[:1])
        at = pl.ds(k * KPAD, KPAD)
        new = (
            jnp.maximum(colour[at, :] - step * grad[k * KPAD : (k + 1) * KPAD], 0.0)
            * alive[k : k + 1, :]
        )
        fresh[at, :] = new
    if last:
        _, h = band_place()
        for c in range(out.shape[0]):
            for k in range(4):
                out[c, pl.ds(k ^ (2 * h), 1), :] = fresh[pl.ds(k * KPAD + c, 1), :]
    else:
        table[...] = colour_table(member, fresh[...])


def update_kernel(p0, r1, r2, r3, own, ablk, out):
    x, _ = band_place()
    quarter = (p0.shape[0] - EXTRA) // 2
    total = p0[...] + r1[...] + r2[...] + r3[...]
    at = pl.ds(pl.multiple_of(x * quarter, quarter), quarter)
    ab = ablk[at, :]
    eye = iota((quarter, quarter), 0) == iota((quarter, quarter), 1)
    for k2 in range(2):
        row = total[2 * quarter + 1 + k2 : 2 * quarter + 2 + k2]
        power = jnp.sum(jnp.where(eye, row, 0.0), axis=1, keepdims=True)
        step = 1.0 / (1.0 + power)
        g = total[k2 * quarter : (k2 + 1) * quarter]
        out[pl.ds(k2 * quarter, quarter), :] = (
            jnp.maximum(own[k2, at, :] - step * g, 0.0) * ab[:, k2 : k2 + 1]
        )
    out[pl.ds(2 * quarter, EXTRA), :] = total[2 * quarter :]


def leave_kernel(n0, r1, r2, r3, table, sent, pair, message_far, message):
    x, _ = band_place()
    quarter = (n0.shape[0] - EXTRA) // 2
    for step, piece in enumerate((n0, r1, r2, r3)):
        q = lax.rem(x + 4 - step, 4)
        at = pl.ds(pl.multiple_of(q * quarter, quarter), quarter)
        for k2 in range(2):
            pair[k2, at, :] = piece[pl.ds(k2 * quarter, quarter), :]
    take = slots_by_block(sent[0], 4 * quarter)
    write_message(message, [pick(take, pair[0]), pick(take, pair[1])], pick(take, table[...]))
    pltpu.sync_copy(message, message_far)


def finish_kernel(n0, r1, r2, r3, m0, m1, m2, m3, lengths, shape, misfit):
    x, h = band_place()
    quarter = (n0.shape[0] - EXTRA) // 2
    total = jnp.zeros((8, lengths.shape[1]), F32)
    for step, (mine, theirs) in enumerate(((n0, m0), (r1, m1), (r2, m2), (r3, m3))):
        q = lax.rem(x + 4 - step, 4)
        at = pl.ds(pl.multiple_of(q * quarter, quarter), quarter)
        for k2 in range(2):
            shape[k2 + 2 * h, at, :] = mine[pl.ds(k2 * quarter, quarter), :]
            shape[k2 + 2 * (1 - h), at, :] = theirs[pl.ds(k2 * quarter, quarter), :]
        ms = mine[pl.ds(2 * quarter, EXTRA), :]
        part = membership_of(lengths[...], quarter, q * quarter)
        hi, lo = halves(ms)
        total = total + lax.dot_general(hi, part, NN, preferred_element_type=F32)
        total = total + lax.dot_general(lo, part, NN, preferred_element_type=F32)
    misfit[...] = total[:1]


def call(kernel, outs, args, scratch=(), limit=54_000_000, cost=3e6, far_in=(), far_out=()):
    many = isinstance(outs, list)
    shapes = [
        s if isinstance(s, jax.ShapeDtypeStruct) else jax.ShapeDtypeStruct(s, F32)
        for s in (outs if many else [outs])
    ]
    near = pl.BlockSpec(memory_space=pltpu.VMEM)
    far = pl.BlockSpec(memory_space=pltpu.HBM)
    got = pl.pallas_call(
        kernel,
        out_shape=shapes,
        in_specs=[far if i in far_in else near for i in range(len(args))],
        out_specs=[far if i in far_out else near for i in range(len(shapes))],
        scratch_shapes=list(scratch),
        compiler_params=pltpu.CompilerParams(vmem_limit_bytes=limit),
        cost_estimate=pl.CostEstimate(flops=0, bytes_accessed=int(cost), transcendentals=0),
    )(*args)
    return got if many else got[0]


def on_device(
    observed, weights, morphology, spectra, blend_blocks, source_count, sent_blocks, landing_blocks
):
    channels, blocks, pixels = observed.shape
    spectra = spectra.transpose(1, 0, 2)
    sent_blocks = sent_blocks.transpose(0, 2, 1)
    landing_blocks = landing_blocks.transpose(0, 2, 1)
    blends = spectra.shape[2]
    peers = sent_blocks.shape[2]
    slots = 4 * peers
    quarter = blocks // 4
    piece = (2 * quarter + EXTRA, pixels)
    pair = (2, blocks, pixels)
    message = (peers * ROWS, pixels)
    band = lax.axis_size("band")

    def over_core(v):
        return lax.ppermute(v, "band", [(i, i ^ 1) for i in range(band)])

    def over_x(v, step):
        return lax.ppermute(v, "band", [(i, (i + 2 * step) % band) for i in range(band)])

    def over_tile(v):
        v = v.reshape(peers, ROWS // 2, 2, pixels)
        return lax.all_to_all(v, "tile", 0, 0, tiled=True).reshape(message)

    counts = source_count.reshape(1, blends)
    colour_rows = (4 * KPAD, blends)
    table_rows = (blocks, 128)

    def kept(v):
        return jax.ShapeDtypeStruct(v.shape, v.dtype)

    def dma(n):
        return pltpu.SemaphoreType.DMA((n,))

    cube = pltpu.VMEM(observed.shape, F32)
    leaving = call(
        first_kernel,
        message,
        (morphology, spectra, blend_blocks, counts, sent_blocks),
        scratch=(
            pltpu.VMEM(pair, F32),
            pltpu.VMEM(spectra.shape, F32),
            pltpu.VMEM(blend_blocks.shape, jnp.int32),
            pltpu.VMEM(counts.shape, jnp.int32),
            pltpu.VMEM(sent_blocks.shape, jnp.int32),
            pltpu.VMEM(colour_rows, F32),
            pltpu.VMEM(message, F32),
            dma(5),
        ),
        limit=67_043_328,
        far_in=range(5),
        far_out=(0,),
    )
    tiles = blocks // 128
    own, other, colour, alive, table, ablk, lengths, sent, land, wide, resid = call(
        start_kernel,
        [
            pair,
            pair,
            colour_rows,
            (8, blends),
            table_rows,
            table_rows,
            kept(blend_blocks),
            kept(sent_blocks),
            kept(landing_blocks),
            (8, blocks),
            observed.shape,
        ],
        (
            morphology,
            spectra,
            blend_blocks,
            counts,
            sent_blocks,
            landing_blocks,
            observed,
        ),
        scratch=(
            pltpu.VMEM(morphology.shape, F32),
            pltpu.VMEM(spectra.shape, F32),
            pltpu.VMEM(counts.shape, jnp.int32),
            cube,
            cube,
            dma(6),
            dma(tiles),
            dma(tiles),
        ),
        cost=20e6,
        limit=67_043_328,
        far_in=range(7),
        far_out=(10,),
    )
    for iteration in range(ITERS):
        last = iteration == ITERS - 1
        mine = over_tile(leaving)
        if iteration:
            wide, resid = call(
                model_kernel,
                [(8, blocks), observed.shape],
                (table, own, other, colour, lengths, observed),
                scratch=(cube, cube, dma(tiles), dma(tiles)),
                cost=16e6,
                far_in=(5,),
                far_out=(1,),
            )
        mine, resid = lax.optimization_barrier((mine, resid))
        partner = over_core(mine)
        wgt, bkeep, bsend, miss = call(
            functools.partial(link_kernel, last),
            [observed.shape, message, message, (8, blocks)],
            (mine, partner, resid, weights, land),
            scratch=(
                pltpu.VMEM((4, slots, pixels), F32),
                pltpu.VMEM((4, slots, pixels), F32),
                pltpu.VMEM((blocks, slots), BF16),
                pltpu.VMEM((slots, blocks), BF16),
                pltpu.VMEM((blocks, pixels), F32),
                cube,
                cube,
                cube,
                dma(channels),
                dma(channels),
                dma(channels),
            ),
            cost=14e6,
            far_in=(2, 3),
            far_out=(0,),
        )
        returning = bkeep + over_core(bsend)
        back = over_tile(returning)
        gkeep, gsend = call(
            grad_kernel,
            [(4,) + piece, (4,) + piece],
            (table, wgt, wide, miss, returning),
            scratch=(cube, dma(tiles)),
            cost=16e6,
            far_in=(1, 4),
        )
        gcame = over_core(gsend)
        p0, p1, p2, p3 = call(
            merge_kernel,
            [piece] * 4,
            (back, gkeep, gcame, sent),
            scratch=(pltpu.VMEM(pair, F32),),
            limit=SMALL,
        )
        r1, r2, r3 = (over_x(v, s) for s, v in ((1, p1), (2, p2), (3, p3)))
        per_block = call(
            product_kernel,
            table_rows,
            (own, other, wgt),
            scratch=(cube, dma(tiles)),
            cost=16e6,
            far_in=(2,),
        )
        colour_args = (back, sent, per_block, lengths, own, other, colour, alive)
        if last:
            new_colour = call(
                functools.partial(colour_kernel, True),
                (channels, 4, blends),
                colour_args,
                scratch=(pltpu.VMEM(colour_rows, F32),),
                limit=SMALL,
                cost=8e6,
            )
        else:
            colour, table = call(
                functools.partial(colour_kernel, False),
                [colour_rows, table_rows],
                colour_args,
                limit=SMALL,
                cost=8e6,
            )
        n0 = call(update_kernel, piece, (p0, r1, r2, r3, own, ablk), limit=SMALL)
        n1, n2, n3 = (over_x(n0, s) for s in (1, 2, 3))
        if not last:
            own, leaving = call(
                leave_kernel, [pair, message], (n0, n1, n2, n3, table, sent),
                scratch=(pltpu.VMEM(message, F32),),
                limit=SMALL,
                far_out=(1,),
            )
            other = over_core(own)
    m0, m1, m2, m3 = (over_core(v) for v in (n0, n1, n2, n3))
    shape, misfit = call(
        finish_kernel,
        [morphology.shape, (1, blends)],
        (n0, n1, n2, n3, m0, m1, m2, m3, lengths),
        limit=SMALL,
    )
    return shape, new_colour.transpose(1, 0, 2), misfit.reshape(blends)


def solution(mesh):
    return jax.shard_map(
        on_device,
        mesh=mesh,
        in_specs=(
            P("band", "tile", None),
            P("band", "tile", None),
            P(None, "tile", None),
            P(None, "band", "tile"),
            P("tile", None),
            P("tile"),
            P("tile", None, None),
            P("tile", None, None),
        ),
        out_specs=(P(None, "tile", None), P(None, "band", "tile"), P("tile")),
        check_vma=False,
    )
```

```python
import functools

import jax
import jax.numpy as jnp
from jax import lax
from jax.experimental import pallas as pl
from jax.experimental.pallas import tpu as pltpu
from jax.sharding import PartitionSpec as P


ITERS = 2
F32 = jnp.float32
BF16 = jnp.bfloat16
HIGH = lax.Precision.HIGHEST
KPAD = 16
ROWS = 10
GROUP = 6
SMALL = 8 << 20
EXTRA = 8
NN = (((1,), (0,)), ((), ()))
NT = (((1,), (1,)), ((), ()))
TN = (((0,), (0,)), ((), ()))


def halves(x):
    hi = x.astype(BF16)
    return hi, (x - hi.astype(F32)).astype(BF16)


def pick(onehot, x, dims=NN):
    n = x.shape[1]
    both = jnp.concatenate(halves(x), axis=1)
    y = lax.dot_general(onehot, both, dims, preferred_element_type=F32)
    return y[:, :n] + y[:, n:]


def exact(a, b, dims):
    return lax.dot_general(a, b, dims, precision=HIGH, preferred_element_type=F32)


def iota(shape, dim):
    return lax.broadcasted_iota(jnp.int32, shape, dim)


def hot(mask):
    return jnp.where(mask, 1.0, 0.0).astype(BF16)


def slot_row(idx):
    cap, peers = idx.shape
    slots = cap * peers
    spread = hot(iota((peers, slots), 1) % peers == iota((peers, slots), 0))
    hi, lo = halves(idx.astype(F32))
    wide = jnp.dot(hi, spread, preferred_element_type=F32) + jnp.dot(
        lo, spread, preferred_element_type=F32
    )
    own = iota((cap, slots), 1) // peers == iota((cap, slots), 0)
    return jnp.sum(jnp.where(own, wide, 0.0), axis=0, keepdims=True)


def slot_column(idx):
    row = slot_row(idx)
    n = row.shape[1]
    return jnp.sum(jnp.where(iota((n, n), 0) == iota((n, n), 1), row, 0.0), axis=1, keepdims=True)


def slots_by_block(idx, blocks):
    slots = idx.shape[0] * idx.shape[1]
    return hot(slot_column(idx) == iota((slots, blocks), 1).astype(F32))


def blocks_by_slot(idx, blocks):
    slots = idx.shape[0] * idx.shape[1]
    return hot(slot_row(idx) == iota((blocks, slots), 0).astype(F32))


def membership_of(lengths, blocks, first=0):
    n = lengths.shape[1]
    upto = hot(iota((n, n), 0) <= iota((n, n), 1))
    rows = jnp.broadcast_to(lengths.astype(F32), (8, n))
    ends = lax.dot_general(rows.astype(BF16), upto, NN, preferred_element_type=F32)[:1]
    starts = ends - lengths.astype(F32)
    position = (iota((blocks, n), 0) + first).astype(F32)
    return hot((position >= starts) & (position < ends))


def band_place():
    me = lax.axis_index("band")
    return me // 2, me % 2


def write_message(out, leaving, colours):
    peers = out.shape[0] // ROWS
    lane = iota((peers, 128), 1)
    for k2 in range(2):
        for j in range(4):
            out[pl.ds(k2 * 4 + j, peers, stride=ROWS), :] = leaving[k2][j * peers : (j + 1) * peers]
    for jj in range(2):
        low = colours[jj * peers : (jj + 1) * peers]
        high = colours[(jj + 2) * peers : (jj + 3) * peers]
        out[pl.ds(8 + jj, peers, stride=ROWS), :] = jnp.where(lane < 64, low, high)


def colour_table(member, colour):
    twice = jnp.concatenate([colour, colour], axis=0)
    hi, lo = halves(twice)
    mid = lax.dot_general(member, hi, NT, preferred_element_type=F32)
    return mid + lax.dot_general(member, lo, NT, preferred_element_type=F32)


def started(copies):
    for c in copies:
        c.start()
    return copies


def begin(spectra, lengths, counts, colour, blocks):
    _, h = band_place()
    channels, _, blends = spectra.shape
    member = membership_of(lengths[...], blocks)
    rel = iota((8, blends), 0)
    absolute = jnp.where(rel < 4, rel ^ (2 * h), 8)
    live = jnp.where(absolute < counts[...], 1.0, 0.0).astype(F32)
    colour[...] = jnp.zeros(colour.shape, F32)
    for c in range(channels):
        for k in range(4):
            colour[pl.ds(k * KPAD + c, 1), :] = spectra[c, pl.ds(k ^ (2 * h), 1), :]
    for k in range(4):
        at = pl.ds(k * KPAD, KPAD)
        colour[at, :] = colour[at, :] * live[k : k + 1]
    wide = jnp.concatenate([live, jnp.zeros((120, blends), F32)], axis=0).astype(BF16)
    ab = lax.dot_general(member, wide, NT, preferred_element_type=F32)
    return member, live, ab, colour_table(member, colour[...])


def first_kernel(
    morph_far,
    spectra_far,
    lengths_far,
    counts_far,
    sent_far,
    message_far,
    morph,
    spectra,
    lengths,
    counts,
    sent,
    colour,
    message,
    sems,
):
    _, h = band_place()
    near = (lengths, counts, spectra, sent, morph)
    far = (lengths_far, counts_far, spectra_far, sent_far, morph_far.at[pl.ds(2 * h, 2)])
    arrivals = started(
        [pltpu.make_async_copy(f, n, sems.at[i]) for i, (f, n) in enumerate(zip(far, near))]
    )
    blocks = morph.shape[1]
    for c in arrivals[:3]:
        c.wait()
    _, _, ab, table = begin(spectra, lengths, counts, colour, blocks)
    for c in arrivals[3:]:
        c.wait()
    take = slots_by_block(sent[0], blocks)
    leaving = [pick(take, morph[k2] * ab[:, k2 : k2 + 1]) for k2 in range(2)]
    write_message(message, leaving, pick(take, table))
    pltpu.sync_copy(message, message_far)


def powers(colour, member):
    sq = colour * colour
    rows8 = iota((8, sq.shape[1]), 0)
    power = jnp.zeros((8, sq.shape[1]), F32)
    for k in range(4):
        total = jnp.sum(sq[k * KPAD : (k + 1) * KPAD], axis=0, keepdims=True)
        power = jnp.where(rows8 == k, total, power)
    hi, lo = halves(power)
    return lax.dot_general(hi, member, NT, preferred_element_type=F32) + lax.dot_general(
        lo, member, NT, preferred_element_type=F32
    )


def tile_copies(far, near, sems, out=False):
    def copy(t):
        there = slice(None), pl.ds(pl.multiple_of(t * 128, 128), 128)
        ends = (near.at[there], far.at[there]) if out else (far.at[there], near.at[there])
        return pltpu.make_async_copy(*ends, sems.at[t])

    return copy


def model_loop(table, own, other, observed, out, arrival, leaving):
    channels, blocks, _ = observed.shape

    def tile(t, carry):
        arrival(t).wait()
        rows = pl.ds(pl.multiple_of(t * 128, 128), 128)
        cb = table[rows, :]
        sh = [own[0, rows, :], own[1, rows, :], other[0, rows, :], other[1, rows, :]]
        for c in range(channels):
            m = sh[0] * cb[:, c : c + 1]
            for k in range(1, 4):
                m = m + sh[k] * cb[:, k * KPAD + c : k * KPAD + c + 1]
            out[c, rows, :] = m - observed[c, rows, :]
        leaving(t).start()
        return carry

    lax.fori_loop(0, blocks // 128, tile, 0)


def start_kernel(
    morph_far,
    spectra_far,
    lengths_far,
    counts_far,
    sent_far,
    land_far,
    observed_far,
    own_far,
    other_far,
    colour,
    alive,
    table,
    ablk,
    lengths,
    sent,
    land,
    wide,
    resid_far,
    own,
    other,
    morph,
    spectra,
    counts,
    observed,
    resid,
    sems,
    sem_in,
    sem_out,
    sem_pair,
):
    _, h = band_place()
    near = (lengths, counts, spectra, sent, land, morph)
    far = (lengths_far, counts_far, spectra_far, sent_far, land_far, morph_far)
    arrivals = started(
        [pltpu.make_async_copy(f, n, sems.at[i]) for i, (f, n) in enumerate(zip(far, near))]
    )
    arrival = tile_copies(observed_far, observed, sem_in)
    leaving = tile_copies(resid_far, resid, sem_out, out=True)
    blocks = own.shape[1]
    tiles = range(blocks // 128)
    started([arrival(t) for t in tiles])
    for c in arrivals[:3]:
        c.wait()
    member, live, ab, rows = begin(spectra, lengths, counts, colour, blocks)
    alive[...] = live
    ablk[...] = ab
    table[...] = rows
    for c in arrivals[3:]:
        c.wait()
    for k2 in range(2):
        own[k2] = morph[k2 ^ (2 * h)] * ab[:, k2 : k2 + 1]
        other[k2] = morph[(k2 + 2) ^ (2 * h)] * ab[:, k2 + 2 : k2 + 3]
    gone = started(
        [
            pltpu.make_async_copy(own, own_far, sem_pair.at[0]),
            pltpu.make_async_copy(other, other_far, sem_pair.at[1]),
        ]
    )
    wide[...] = powers(colour[...], member)
    model_loop(table, own, other, observed, resid, arrival, leaving)
    for c in gone:
        c.wait()
    for t in tiles:
        leaving(t).wait()


def model_kernel(
    table,
    own,
    other,
    colour,
    lengths,
    observed_far,
    wide,
    resid_far,
    observed,
    resid,
    sem_in,
    sem_out,
):
    arrival = tile_copies(observed_far, observed, sem_in)
    leaving = tile_copies(resid_far, resid, sem_out, out=True)
    blocks = own.shape[1]
    tiles = range(blocks // 128)
    started([arrival(t) for t in tiles])
    wide[...] = powers(colour[...], membership_of(lengths[...], blocks))
    model_loop(table, own, other, observed, resid, arrival, leaving)
    for t in tiles:
        leaving(t).wait()


def link_kernel(
    last,
    mine,
    partner,
    resid_far,
    weights_far,
    land,
    wout_far,
    keep,
    send,
    miss,
    shs,
    back,
    sbs,
    ssb,
    macc,
    resid,
    weights,
    wout,
    sem_r,
    sem_w,
    sem_out,
):
    channels, blocks, pixels = resid.shape
    peers = land.shape[2]
    slots = 4 * peers

    def arrivals(c):
        return (
            pltpu.make_async_copy(resid_far.at[c], resid.at[c], sem_r.at[c]),
            pltpu.make_async_copy(weights_far.at[c], weights.at[c], sem_w.at[c]),
        )

    def gone(c):
        return pltpu.make_async_copy(wout.at[c], wout_far.at[c], sem_out.at[c])

    for c in range(GROUP):
        started(arrivals(c))
    sbs[...] = blocks_by_slot(land[0], blocks)
    ssb[...] = slots_by_block(land[0], blocks)
    for k2 in range(2):
        for j in range(4):
            rows = pl.ds(j * peers, peers)
            shs[k2, rows, :] = mine[pl.ds(k2 * 4 + j, peers, stride=ROWS), :]
            shs[k2 + 2, rows, :] = partner[pl.ds(k2 * 4 + j, peers, stride=ROWS), :]
    back[...] = jnp.zeros(back.shape, F32)
    if last:
        macc[...] = jnp.zeros(macc.shape, F32)
    lane = iota((peers, 128), 1)

    def group(g, carry):
        ci, bc = carry[:2], list(carry[2:])

        @pl.when(g + 1 < channels // GROUP)
        def _():
            for u in range(GROUP):
                started(arrivals((g + 1) * GROUP + u))

        for u in range(GROUP):
            for a in arrivals(g * GROUP + u):
                a.wait()
        for u in range(GROUP):
            c = g * GROUP + u
            parts = []
            for j in range(4):
                rows = pl.ds(j * peers, peers)
                at = u + (64 if j >= 2 else 0)
                m = shs[0, rows, :] * ci[j % 2][:, at : at + 1]
                for k in range(1, 4):
                    col = at + k * KPAD
                    m = m + shs[k, rows, :] * ci[j % 2][:, col : col + 1]
                parts.append(m)
            both = jnp.concatenate(halves(jnp.concatenate(parts, axis=0)), axis=1)
            landed = jnp.zeros((slots, 2 * pixels), F32)
            for q in range(blocks // 128):
                rows = pl.ds(q * 128, 128)
                y = jnp.dot(sbs[rows, :], both, preferred_element_type=F32)
                x = resid[c, rows, :] + (y[:, :pixels] + y[:, pixels:])
                wt = weights[c, rows, :] * x
                wout[c, rows, :] = wt
                if last:
                    macc[rows, :] += wt * x
                wboth = jnp.concatenate(halves(wt), axis=1)
                landed = landed + jnp.dot(ssb[:, rows], wboth, preferred_element_type=F32)
            landed = landed[:, :pixels] + landed[:, pixels:]
            for j in range(4):
                rows = pl.ds(j * peers, peers)
                at = u + (64 if j >= 2 else 0)
                ld = landed[j * peers : (j + 1) * peers]
                for k in range(4):
                    col = at + k * KPAD
                    back[k, rows, :] += ci[j % 2][:, col : col + 1] * ld
                    r = jnp.sum(shs[k, rows, :] * ld, axis=1, keepdims=True)
                    bc[j % 2] = jnp.where(lane == col, r, bc[j % 2])
        for u in range(GROUP):
            gone(g * GROUP + u).start()
        return tuple(pltpu.roll(v, 128 - GROUP, 1) for v in (*ci, *bc))

    ci = tuple(mine[pl.ds(8 + jj, peers, stride=ROWS), :] for jj in range(2))
    none = jnp.zeros((peers, 128), F32)
    done = lax.fori_loop(0, channels // GROUP, group, (*ci, none, none))
    bc = [pltpu.roll(v, channels, 1) for v in done[2:]]
    keep[...] = jnp.zeros(keep.shape, F32)
    send[...] = jnp.zeros(send.shape, F32)
    for k2 in range(2):
        for j in range(4):
            rows = pl.ds(j * peers, peers)
            keep[pl.ds(k2 * 4 + j, peers, stride=ROWS), :] = back[k2, rows, :]
            send[pl.ds(k2 * 4 + j, peers, stride=ROWS), :] = back[k2 + 2, rows, :]
    for jj in range(2):
        keep[pl.ds(8 + jj, peers, stride=ROWS), :] = bc[jj]
    if last:
        miss[...] = exact(jnp.ones((8, pixels), F32), macc[...], NT)
    else:
        miss[...] = jnp.zeros(miss.shape, F32)
    for c in range(channels):
        gone(c).wait()


def grad_kernel(table, wgt_far, wide, miss, after, keep, send, wgt, sems):
    channels, blocks, _ = wgt.shape
    quarter = blocks // 4
    arrival = tile_copies(wgt_far, wgt, sems)
    started([arrival(t) for t in range(4)])
    for q in range(4):
        w = wide[:, q * quarter : (q + 1) * quarter]
        m = miss[0:1, q * quarter : (q + 1) * quarter]
        r = iota((8, quarter), 0)
        first = jnp.where(r == 0, m, jnp.where(r == 1, w[0:1], jnp.where(r == 2, w[1:2], 0.0)))
        second = jnp.where(r == 0, m, jnp.where(r == 1, w[2:3], jnp.where(r == 2, w[3:4], 0.0)))
        keep[q, pl.ds(2 * quarter, EXTRA), :] = first
        send[q, pl.ds(2 * quarter, EXTRA), :] = second

    def shapes(q, carry):
        arrival(q).wait()
        for half in range(2):
            rows = pl.ds(pl.multiple_of(q * quarter + half * 64, 64), 64)
            cb = table[rows, :]
            gs = [None] * 4
            for c in range(channels):
                wt = wgt[c, rows, :]
                for k in range(4):
                    term = cb[:, k * KPAD + c : k * KPAD + c + 1] * wt
                    gs[k] = term if c == 0 else gs[k] + term
            for k2 in range(2):
                keep[q, pl.ds(k2 * quarter + half * 64, 64), :] = gs[k2]
                send[q, pl.ds(k2 * quarter + half * 64, 64), :] = gs[k2 + 2]
        return carry

    lax.fori_loop(0, 4, shapes, 0)


def product_kernel(own, other, wgt_far, per_block, wgt, sems):
    channels, blocks, _ = wgt.shape
    lane = iota((128, 128), 1)
    arrival = tile_copies(wgt_far, wgt, sems)
    started([arrival(t) for t in range(blocks // 128)])

    def tile(t, carry):
        arrival(t).wait()
        rows = pl.ds(pl.multiple_of(t * 128, 128), 128)
        sh = [own[0, rows, :], own[1, rows, :], other[0, rows, :], other[1, rows, :]]
        pb = jnp.zeros((128, 128), F32)
        for c in range(channels):
            wt = wgt[c, rows, :]
            for k in range(4):
                r = jnp.sum(sh[k] * wt, axis=1, keepdims=True)
                pb = jnp.where(lane == k * KPAD + c, r, pb)
        per_block[rows, :] = pb
        return carry

    lax.fori_loop(0, blocks // 128, tile, 0)


def merge_kernel(arrived, keep, came, sent, p0, p1, p2, p3, scat):
    x, _ = band_place()
    peers = sent.shape[2]
    quarter = (p0.shape[0] - EXTRA) // 2
    blocks = 4 * quarter
    put = blocks_by_slot(sent[0], blocks)
    for k2 in range(2):
        rows = [arrived[pl.ds(k2 * 4 + j, peers, stride=ROWS), :] for j in range(4)]
        scat[k2] = pick(put, jnp.concatenate(rows, axis=0))
    for step, out in enumerate((p0, p1, p2, p3)):
        q = lax.rem(x + step, 4)
        out[...] = keep[q] + came[q]
        for k2 in range(2):
            at = pl.ds(pl.multiple_of(q * quarter, quarter), quarter)
            out[pl.ds(k2 * quarter, quarter), :] += scat[k2, at, :]


def colour_kernel(
    last, arrived, sent, per_block, lengths, own, other, colour, alive, *outs
):
    if last:
        out, fresh = outs
    else:
        fresh, table = outs
    blocks = per_block.shape[0]
    peers = sent.shape[2]
    member = membership_of(lengths[...], blocks)
    put = blocks_by_slot(sent[0], blocks)
    lane = iota((peers, 128), 1)
    rows = []
    for j in range(4):
        row = arrived[pl.ds(8 + j % 2, peers, stride=ROWS), :]
        rows.append(jnp.where((lane < 64) == (j < 2), row, 0.0))
    total = per_block[...] + pick(put, jnp.concatenate(rows, axis=0))
    hi, lo = halves(total)
    grad = lax.dot_general(hi, member, TN, preferred_element_type=F32) + lax.dot_general(
        lo, member, TN, preferred_element_type=F32
    )
    grad = grad[:64] + grad[64:]
    ones = jnp.ones((8, own.shape[2]), F32)
    for k in range(4):
        s = own[k] if k < 2 else other[k - 2]
        by_block = exact(ones, s * s, NT)
        hi, lo = halves(by_block)
        power = lax.dot_general(hi, member, NN, preferred_element_type=F32) + lax.dot_general(
            lo, member, NN, preferred_element_type=F32
        )
        step = 1.0 / (1.0 + power[:1])
        at = pl.ds(k * KPAD, KPAD)
        new = (
            jnp.maximum(colour[at, :] - step * grad[k * KPAD : (k + 1) * KPAD], 0.0)
            * alive[k : k + 1, :]
        )
        fresh[at, :] = new
    if last:
        _, h = band_place()
        for c in range(out.shape[0]):
            for k in range(4):
                out[c, pl.ds(k ^ (2 * h), 1), :] = fresh[pl.ds(k * KPAD + c, 1), :]
    else:
        table[...] = colour_table(member, fresh[...])


def update_kernel(p0, r1, r2, r3, own, ablk, out):
    x, _ = band_place()
    quarter = (p0.shape[0] - EXTRA) // 2
    total = p0[...] + r1[...] + r2[...] + r3[...]
    at = pl.ds(pl.multiple_of(x * quarter, quarter), quarter)
    ab = ablk[at, :]
    eye = iota((quarter, quarter), 0) == iota((quarter, quarter), 1)
    for k2 in range(2):
        row = total[2 * quarter + 1 + k2 : 2 * quarter + 2 + k2]
        power = jnp.sum(jnp.where(eye, row, 0.0), axis=1, keepdims=True)
        step = 1.0 / (1.0 + power)
        g = total[k2 * quarter : (k2 + 1) * quarter]
        out[pl.ds(k2 * quarter, quarter), :] = (
            jnp.maximum(own[k2, at, :] - step * g, 0.0) * ab[:, k2 : k2 + 1]
        )
    out[pl.ds(2 * quarter, EXTRA), :] = total[2 * quarter :]


def leave_kernel(n0, r1, r2, r3, table, sent, pair, message_far, message):
    x, _ = band_place()
    quarter = (n0.shape[0] - EXTRA) // 2
    for step, piece in enumerate((n0, r1, r2, r3)):
        q = lax.rem(x + 4 - step, 4)
        at = pl.ds(pl.multiple_of(q * quarter, quarter), quarter)
        for k2 in range(2):
            pair[k2, at, :] = piece[pl.ds(k2 * quarter, quarter), :]
    take = slots_by_block(sent[0], 4 * quarter)
    write_message(message, [pick(take, pair[0]), pick(take, pair[1])], pick(take, table[...]))
    pltpu.sync_copy(message, message_far)


def finish_kernel(n0, r1, r2, r3, m0, m1, m2, m3, lengths, shape, misfit):
    x, h = band_place()
    quarter = (n0.shape[0] - EXTRA) // 2
    total = jnp.zeros((8, lengths.shape[1]), F32)
    for step, (mine, theirs) in enumerate(((n0, m0), (r1, m1), (r2, m2), (r3, m3))):
        q = lax.rem(x + 4 - step, 4)
        at = pl.ds(pl.multiple_of(q * quarter, quarter), quarter)
        for k2 in range(2):
            shape[k2 + 2 * h, at, :] = mine[pl.ds(k2 * quarter, quarter), :]
            shape[k2 + 2 * (1 - h), at, :] = theirs[pl.ds(k2 * quarter, quarter), :]
        ms = mine[pl.ds(2 * quarter, EXTRA), :]
        part = membership_of(lengths[...], quarter, q * quarter)
        hi, lo = halves(ms)
        total = total + lax.dot_general(hi, part, NN, preferred_element_type=F32)
        total = total + lax.dot_general(lo, part, NN, preferred_element_type=F32)
    misfit[...] = total[:1]


def call(kernel, outs, args, scratch=(), limit=54_000_000, cost=3e6, far_in=(), far_out=()):
    many = isinstance(outs, list)
    shapes = [
        s if isinstance(s, jax.ShapeDtypeStruct) else jax.ShapeDtypeStruct(s, F32)
        for s in (outs if many else [outs])
    ]
    near = pl.BlockSpec(memory_space=pltpu.VMEM)
    far = pl.BlockSpec(memory_space=pltpu.HBM)
    got = pl.pallas_call(
        kernel,
        out_shape=shapes,
        in_specs=[far if i in far_in else near for i in range(len(args))],
        out_specs=[far if i in far_out else near for i in range(len(shapes))],
        scratch_shapes=list(scratch),
        compiler_params=pltpu.CompilerParams(vmem_limit_bytes=limit),
        cost_estimate=pl.CostEstimate(flops=0, bytes_accessed=int(cost), transcendentals=0),
    )(*args)
    return got if many else got[0]


def on_device(
    observed, weights, morphology, spectra, blend_blocks, source_count, sent_blocks, landing_blocks
):
    channels, blocks, pixels = observed.shape
    spectra = spectra.transpose(1, 0, 2)
    sent_blocks = sent_blocks.transpose(0, 2, 1)
    landing_blocks = landing_blocks.transpose(0, 2, 1)
    blends = spectra.shape[2]
    peers = sent_blocks.shape[2]
    slots = 4 * peers
    quarter = blocks // 4
    piece = (2 * quarter + EXTRA, pixels)
    pair = (2, blocks, pixels)
    message = (peers * ROWS, pixels)
    band = lax.axis_size("band")

    def over_core(v):
        return lax.ppermute(v, "band", [(i, i ^ 1) for i in range(band)])

    def over_x(v, step):
        return lax.ppermute(v, "band", [(i, (i + 2 * step) % band) for i in range(band)])

    def over_tile(v):
        v = v.reshape(peers, ROWS // 2, 2, pixels)
        return lax.all_to_all(v, "tile", 0, 0, tiled=True).reshape(message)

    counts = source_count.reshape(1, blends)
    colour_rows = (4 * KPAD, blends)
    table_rows = (blocks, 128)

    def kept(v):
        return jax.ShapeDtypeStruct(v.shape, v.dtype)

    def dma(n):
        return pltpu.SemaphoreType.DMA((n,))

    cube = pltpu.VMEM(observed.shape, F32)
    leaving = call(
        first_kernel,
        message,
        (morphology, spectra, blend_blocks, counts, sent_blocks),
        scratch=(
            pltpu.VMEM(pair, F32),
            pltpu.VMEM(spectra.shape, F32),
            pltpu.VMEM(blend_blocks.shape, jnp.int32),
            pltpu.VMEM(counts.shape, jnp.int32),
            pltpu.VMEM(sent_blocks.shape, jnp.int32),
            pltpu.VMEM(colour_rows, F32),
            pltpu.VMEM(message, F32),
            dma(5),
        ),
        limit=67_043_328,
        far_in=range(5),
        far_out=(0,),
    )
    tiles = blocks // 128
    own, other, colour, alive, table, ablk, lengths, sent, land, wide, resid = call(
        start_kernel,
        [
            pair,
            pair,
            colour_rows,
            (8, blends),
            table_rows,
            table_rows,
            kept(blend_blocks),
            kept(sent_blocks),
            kept(landing_blocks),
            (8, blocks),
            observed.shape,
        ],
        (
            morphology,
            spectra,
            blend_blocks,
            counts,
            sent_blocks,
            landing_blocks,
            observed,
        ),
        scratch=(
            pltpu.VMEM(pair, F32),
            pltpu.VMEM(pair, F32),
            pltpu.VMEM(morphology.shape, F32),
            pltpu.VMEM(spectra.shape, F32),
            pltpu.VMEM(counts.shape, jnp.int32),
            cube,
            cube,
            dma(6),
            dma(tiles),
            dma(tiles),
            dma(2),
        ),
        cost=20e6,
        limit=67_043_328,
        far_in=range(7),
        far_out=(0, 1, 10),
    )
    for iteration in range(ITERS):
        last = iteration == ITERS - 1
        mine = over_tile(leaving)
        if iteration:
            wide, resid = call(
                model_kernel,
                [(8, blocks), observed.shape],
                (table, own, other, colour, lengths, observed),
                scratch=(cube, cube, dma(tiles), dma(tiles)),
                cost=16e6,
                far_in=(5,),
                far_out=(1,),
            )
        mine, resid = lax.optimization_barrier((mine, resid))
        partner = over_core(mine)
        wgt, bkeep, bsend, miss = call(
            functools.partial(link_kernel, last),
            [observed.shape, message, message, (8, blocks)],
            (mine, partner, resid, weights, land),
            scratch=(
                pltpu.VMEM((4, slots, pixels), F32),
                pltpu.VMEM((4, slots, pixels), F32),
                pltpu.VMEM((blocks, slots), BF16),
                pltpu.VMEM((slots, blocks), BF16),
                pltpu.VMEM((blocks, pixels), F32),
                cube,
                cube,
                cube,
                dma(channels),
                dma(channels),
                dma(channels),
            ),
            cost=14e6,
            far_in=(2, 3),
            far_out=(0,),
        )
        returning = bkeep + over_core(bsend)
        back = over_tile(returning)
        gkeep, gsend = call(
            grad_kernel,
            [(4,) + piece, (4,) + piece],
            (table, wgt, wide, miss, returning),
            scratch=(cube, dma(tiles)),
            cost=16e6,
            far_in=(1, 4),
        )
        gcame = over_core(gsend)
        p0, p1, p2, p3 = call(
            merge_kernel,
            [piece] * 4,
            (back, gkeep, gcame, sent),
            scratch=(pltpu.VMEM(pair, F32),),
            limit=SMALL,
        )
        r1, r2, r3 = (over_x(v, s) for s, v in ((1, p1), (2, p2), (3, p3)))
        per_block = call(
            product_kernel,
            table_rows,
            (own, other, wgt),
            scratch=(cube, dma(tiles)),
            cost=16e6,
            far_in=(2,),
        )
        colour_args = (back, sent, per_block, lengths, own, other, colour, alive)
        if last:
            new_colour = call(
                functools.partial(colour_kernel, True),
                (channels, 4, blends),
                colour_args,
                scratch=(pltpu.VMEM(colour_rows, F32),),
                limit=SMALL,
                cost=8e6,
            )
        else:
            colour, table = call(
                functools.partial(colour_kernel, False),
                [colour_rows, table_rows],
                colour_args,
                limit=SMALL,
                cost=8e6,
            )
        n0 = call(update_kernel, piece, (p0, r1, r2, r3, own, ablk), limit=SMALL)
        n1, n2, n3 = (over_x(n0, s) for s in (1, 2, 3))
        if not last:
            own, leaving = call(
                leave_kernel, [pair, message], (n0, n1, n2, n3, table, sent),
                scratch=(pltpu.VMEM(message, F32),),
                limit=SMALL,
                far_out=(1,),
            )
            other = over_core(own)
    m0, m1, m2, m3 = (over_core(v) for v in (n0, n1, n2, n3))
    shape, misfit = call(
        finish_kernel,
        [morphology.shape, (1, blends)],
        (n0, n1, n2, n3, m0, m1, m2, m3, lengths),
        limit=SMALL,
    )
    return shape, new_colour.transpose(1, 0, 2), misfit.reshape(blends)


def solution(mesh):
    return jax.shard_map(
        on_device,
        mesh=mesh,
        in_specs=(
            P("band", "tile", None),
            P("band", "tile", None),
            P(None, "tile", None),
            P(None, "band", "tile"),
            P("tile", None),
            P("tile"),
            P("tile", None, None),
            P("tile", None, None),
        ),
        out_specs=(P(None, "tile", None), P(None, "band", "tile"), P("tile")),
        check_vma=False,
    )
```

```python
import functools

import jax
import jax.numpy as jnp
from jax import lax
from jax.experimental import pallas as pl
from jax.experimental.pallas import tpu as pltpu
from jax.sharding import PartitionSpec as P


ITERS = 2
F32 = jnp.float32
BF16 = jnp.bfloat16
HIGH = lax.Precision.HIGHEST
KPAD = 16
ROWS = 10
GROUP = 6
SMALL = 8 << 20
EXTRA = 8
NN = (((1,), (0,)), ((), ()))
NT = (((1,), (1,)), ((), ()))
TN = (((0,), (0,)), ((), ()))


def halves(x):
    hi = x.astype(BF16)
    return hi, (x - hi.astype(F32)).astype(BF16)


def pick(onehot, x, dims=NN):
    n = x.shape[1]
    both = jnp.concatenate(halves(x), axis=1)
    y = lax.dot_general(onehot, both, dims, preferred_element_type=F32)
    return y[:, :n] + y[:, n:]


def exact(a, b, dims):
    return lax.dot_general(a, b, dims, precision=HIGH, preferred_element_type=F32)


def iota(shape, dim):
    return lax.broadcasted_iota(jnp.int32, shape, dim)


def hot(mask):
    return jnp.where(mask, 1.0, 0.0).astype(BF16)


def slot_row(idx):
    cap, peers = idx.shape
    slots = cap * peers
    spread = hot(iota((peers, slots), 1) % peers == iota((peers, slots), 0))
    hi, lo = halves(idx.astype(F32))
    wide = jnp.dot(hi, spread, preferred_element_type=F32) + jnp.dot(
        lo, spread, preferred_element_type=F32
    )
    own = iota((cap, slots), 1) // peers == iota((cap, slots), 0)
    return jnp.sum(jnp.where(own, wide, 0.0), axis=0, keepdims=True)


def slot_column(idx):
    row = slot_row(idx)
    n = row.shape[1]
    return jnp.sum(jnp.where(iota((n, n), 0) == iota((n, n), 1), row, 0.0), axis=1, keepdims=True)


def slots_by_block(idx, blocks):
    slots = idx.shape[0] * idx.shape[1]
    return hot(slot_column(idx) == iota((slots, blocks), 1).astype(F32))


def blocks_by_slot(idx, blocks):
    slots = idx.shape[0] * idx.shape[1]
    return hot(slot_row(idx) == iota((blocks, slots), 0).astype(F32))


def membership_of(lengths, blocks, first=0):
    n = lengths.shape[1]
    upto = hot(iota((n, n), 0) <= iota((n, n), 1))
    rows = jnp.broadcast_to(lengths.astype(F32), (8, n))
    ends = lax.dot_general(rows.astype(BF16), upto, NN, preferred_element_type=F32)[:1]
    starts = ends - lengths.astype(F32)
    position = (iota((blocks, n), 0) + first).astype(F32)
    return hot((position >= starts) & (position < ends))


def band_place():
    me = lax.axis_index("band")
    return me // 2, me % 2


def write_message(out, leaving, colours):
    peers = out.shape[0] // ROWS
    lane = iota((peers, 128), 1)
    for k2 in range(2):
        for j in range(4):
            out[pl.ds(k2 * 4 + j, peers, stride=ROWS), :] = leaving[k2][j * peers : (j + 1) * peers]
    for jj in range(2):
        low = colours[jj * peers : (jj + 1) * peers]
        high = colours[(jj + 2) * peers : (jj + 3) * peers]
        out[pl.ds(8 + jj, peers, stride=ROWS), :] = jnp.where(lane < 64, low, high)


def colour_table(member, colour):
    twice = jnp.concatenate([colour, colour], axis=0)
    hi, lo = halves(twice)
    mid = lax.dot_general(member, hi, NT, preferred_element_type=F32)
    return mid + lax.dot_general(member, lo, NT, preferred_element_type=F32)


def started(copies):
    for c in copies:
        c.start()
    return copies


def begin(spectra, lengths, counts, colour, blocks):
    _, h = band_place()
    channels, _, blends = spectra.shape
    member = membership_of(lengths[...], blocks)
    rel = iota((8, blends), 0)
    absolute = jnp.where(rel < 4, rel ^ (2 * h), 8)
    live = jnp.where(absolute < counts[...], 1.0, 0.0).astype(F32)
    colour[...] = jnp.zeros(colour.shape, F32)
    for c in range(channels):
        for k in range(4):
            colour[pl.ds(k * KPAD + c, 1), :] = spectra[c, pl.ds(k ^ (2 * h), 1), :]
    for k in range(4):
        at = pl.ds(k * KPAD, KPAD)
        colour[at, :] = colour[at, :] * live[k : k + 1]
    wide = jnp.concatenate([live, jnp.zeros((120, blends), F32)], axis=0).astype(BF16)
    ab = lax.dot_general(member, wide, NT, preferred_element_type=F32)
    return member, live, ab, colour_table(member, colour[...])


def first_kernel(
    morph_far,
    spectra_far,
    lengths_far,
    counts_far,
    sent_far,
    message_far,
    morph,
    spectra,
    lengths,
    counts,
    sent,
    colour,
    message,
    sems,
):
    _, h = band_place()
    near = (lengths, counts, spectra, sent, morph)
    far = (lengths_far, counts_far, spectra_far, sent_far, morph_far.at[pl.ds(2 * h, 2)])
    arrivals = started(
        [pltpu.make_async_copy(f, n, sems.at[i]) for i, (f, n) in enumerate(zip(far, near))]
    )
    blocks = morph.shape[1]
    for c in arrivals[:3]:
        c.wait()
    _, _, ab, table = begin(spectra, lengths, counts, colour, blocks)
    for c in arrivals[3:]:
        c.wait()
    take = slots_by_block(sent[0], blocks)
    leaving = [pick(take, morph[k2] * ab[:, k2 : k2 + 1]) for k2 in range(2)]
    write_message(message, leaving, pick(take, table))
    pltpu.sync_copy(message, message_far)


def powers(colour, member):
    sq = colour * colour
    rows8 = iota((8, sq.shape[1]), 0)
    power = jnp.zeros((8, sq.shape[1]), F32)
    for k in range(4):
        total = jnp.sum(sq[k * KPAD : (k + 1) * KPAD], axis=0, keepdims=True)
        power = jnp.where(rows8 == k, total, power)
    hi, lo = halves(power)
    return lax.dot_general(hi, member, NT, preferred_element_type=F32) + lax.dot_general(
        lo, member, NT, preferred_element_type=F32
    )


def tile_copies(far, near, sems, out=False):
    def copy(t):
        there = slice(None), pl.ds(pl.multiple_of(t * 128, 128), 128)
        ends = (near.at[there], far.at[there]) if out else (far.at[there], near.at[there])
        return pltpu.make_async_copy(*ends, sems.at[t])

    return copy


def model_loop(table, own, other, observed, out, arrival, leaving):
    channels, blocks, _ = observed.shape

    def tile(t, carry):
        arrival(t).wait()
        rows = pl.ds(pl.multiple_of(t * 128, 128), 128)
        cb = table[rows, :]
        sh = [own[0, rows, :], own[1, rows, :], other[0, rows, :], other[1, rows, :]]
        for c in range(channels):
            m = sh[0] * cb[:, c : c + 1]
            for k in range(1, 4):
                m = m + sh[k] * cb[:, k * KPAD + c : k * KPAD + c + 1]
            out[c, rows, :] = m - observed[c, rows, :]
        leaving(t).start()
        return carry

    lax.fori_loop(0, blocks // 128, tile, 0)


def start_kernel(
    morph_far,
    spectra_far,
    lengths_far,
    counts_far,
    sent_far,
    land_far,
    observed_far,
    own_out,
    other_out,
    colour_out,
    alive_out,
    table_out,
    ablk_out,
    lengths_out,
    sent_out,
    land_out,
    wide_out,
    resid_far,
    own,
    other,
    colour,
    alive,
    table,
    ablk,
    lengths,
    sent,
    land,
    wide,
    morph,
    spectra,
    counts,
    observed,
    resid,
    sems,
    sem_in,
    sem_out,
    sem_state,
):
    _, h = band_place()
    near = (lengths, counts, spectra, sent, land, morph)
    far = (lengths_far, counts_far, spectra_far, sent_far, land_far, morph_far)
    arrivals = started(
        [pltpu.make_async_copy(f, n, sems.at[i]) for i, (f, n) in enumerate(zip(far, near))]
    )
    arrival = tile_copies(observed_far, observed, sem_in)
    leaving = tile_copies(resid_far, resid, sem_out, out=True)
    blocks = own.shape[1]
    tiles = range(blocks // 128)
    started([arrival(t) for t in tiles])
    for c in arrivals[:3]:
        c.wait()
    member, live, ab, rows = begin(spectra, lengths, counts, colour, blocks)
    alive[...] = live
    ablk[...] = ab
    table[...] = rows
    for c in arrivals[3:]:
        c.wait()
    for k2 in range(2):
        own[k2] = morph[k2 ^ (2 * h)] * ab[:, k2 : k2 + 1]
        other[k2] = morph[(k2 + 2) ^ (2 * h)] * ab[:, k2 + 2 : k2 + 3]
    wide[...] = powers(colour[...], member)
    state = (own, other, colour, alive, table, ablk, lengths, sent, land, wide)
    outs = (
        own_out,
        other_out,
        colour_out,
        alive_out,
        table_out,
        ablk_out,
        lengths_out,
        sent_out,
        land_out,
        wide_out,
    )
    gone = started(
        [pltpu.make_async_copy(v, o, sem_state.at[i]) for i, (v, o) in enumerate(zip(state, outs))]
    )
    model_loop(table, own, other, observed, resid, arrival, leaving)
    for c in gone:
        c.wait()
    for t in tiles:
        leaving(t).wait()


def model_kernel(
    table,
    own,
    other,
    colour,
    lengths,
    observed_far,
    wide,
    resid_far,
    observed,
    resid,
    sem_in,
    sem_out,
):
    arrival = tile_copies(observed_far, observed, sem_in)
    leaving = tile_copies(resid_far, resid, sem_out, out=True)
    blocks = own.shape[1]
    tiles = range(blocks // 128)
    started([arrival(t) for t in tiles])
    wide[...] = powers(colour[...], membership_of(lengths[...], blocks))
    model_loop(table, own, other, observed, resid, arrival, leaving)
    for t in tiles:
        leaving(t).wait()


def link_kernel(
    last,
    mine,
    partner,
    resid_far,
    weights_far,
    land,
    wout_far,
    keep,
    send,
    miss,
    shs,
    back,
    sbs,
    ssb,
    macc,
    resid,
    weights,
    wout,
    sem_r,
    sem_w,
    sem_out,
):
    channels, blocks, pixels = resid.shape
    peers = land.shape[2]
    slots = 4 * peers

    def arrivals(c):
        return (
            pltpu.make_async_copy(resid_far.at[c], resid.at[c], sem_r.at[c]),
            pltpu.make_async_copy(weights_far.at[c], weights.at[c], sem_w.at[c]),
        )

    def gone(c):
        return pltpu.make_async_copy(wout.at[c], wout_far.at[c], sem_out.at[c])

    for c in range(GROUP):
        started(arrivals(c))
    sbs[...] = blocks_by_slot(land[0], blocks)
    ssb[...] = slots_by_block(land[0], blocks)
    for k2 in range(2):
        for j in range(4):
            rows = pl.ds(j * peers, peers)
            shs[k2, rows, :] = mine[pl.ds(k2 * 4 + j, peers, stride=ROWS), :]
            shs[k2 + 2, rows, :] = partner[pl.ds(k2 * 4 + j, peers, stride=ROWS), :]
    back[...] = jnp.zeros(back.shape, F32)
    if last:
        macc[...] = jnp.zeros(macc.shape, F32)
    lane = iota((peers, 128), 1)

    def group(g, carry):
        ci, bc = carry[:2], list(carry[2:])

        @pl.when(g + 1 < channels // GROUP)
        def _():
            for u in range(GROUP):
                started(arrivals((g + 1) * GROUP + u))

        for u in range(GROUP):
            for a in arrivals(g * GROUP + u):
                a.wait()
        for u in range(GROUP):
            c = g * GROUP + u
            parts = []
            for j in range(4):
                rows = pl.ds(j * peers, peers)
                at = u + (64 if j >= 2 else 0)
                m = shs[0, rows, :] * ci[j % 2][:, at : at + 1]
                for k in range(1, 4):
                    col = at + k * KPAD
                    m = m + shs[k, rows, :] * ci[j % 2][:, col : col + 1]
                parts.append(m)
            both = jnp.concatenate(halves(jnp.concatenate(parts, axis=0)), axis=1)
            landed = jnp.zeros((slots, 2 * pixels), F32)
            for q in range(blocks // 128):
                rows = pl.ds(q * 128, 128)
                y = jnp.dot(sbs[rows, :], both, preferred_element_type=F32)
                x = resid[c, rows, :] + (y[:, :pixels] + y[:, pixels:])
                wt = weights[c, rows, :] * x
                wout[c, rows, :] = wt
                if last:
                    macc[rows, :] += wt * x
                wboth = jnp.concatenate(halves(wt), axis=1)
                landed = landed + jnp.dot(ssb[:, rows], wboth, preferred_element_type=F32)
            landed = landed[:, :pixels] + landed[:, pixels:]
            for j in range(4):
                rows = pl.ds(j * peers, peers)
                at = u + (64 if j >= 2 else 0)
                ld = landed[j * peers : (j + 1) * peers]
                for k in range(4):
                    col = at + k * KPAD
                    back[k, rows, :] += ci[j % 2][:, col : col + 1] * ld
                    r = jnp.sum(shs[k, rows, :] * ld, axis=1, keepdims=True)
                    bc[j % 2] = jnp.where(lane == col, r, bc[j % 2])
        for u in range(GROUP):
            gone(g * GROUP + u).start()
        return tuple(pltpu.roll(v, 128 - GROUP, 1) for v in (*ci, *bc))

    ci = tuple(mine[pl.ds(8 + jj, peers, stride=ROWS), :] for jj in range(2))
    none = jnp.zeros((peers, 128), F32)
    done = lax.fori_loop(0, channels // GROUP, group, (*ci, none, none))
    bc = [pltpu.roll(v, channels, 1) for v in done[2:]]
    keep[...] = jnp.zeros(keep.shape, F32)
    send[...] = jnp.zeros(send.shape, F32)
    for k2 in range(2):
        for j in range(4):
            rows = pl.ds(j * peers, peers)
            keep[pl.ds(k2 * 4 + j, peers, stride=ROWS), :] = back[k2, rows, :]
            send[pl.ds(k2 * 4 + j, peers, stride=ROWS), :] = back[k2 + 2, rows, :]
    for jj in range(2):
        keep[pl.ds(8 + jj, peers, stride=ROWS), :] = bc[jj]
    if last:
        miss[...] = exact(jnp.ones((8, pixels), F32), macc[...], NT)
    else:
        miss[...] = jnp.zeros(miss.shape, F32)
    for c in range(channels):
        gone(c).wait()


def grad_kernel(table, wgt_far, wide, miss, after, keep, send, wgt, sems):
    channels, blocks, _ = wgt.shape
    quarter = blocks // 4
    arrival = tile_copies(wgt_far, wgt, sems)
    started([arrival(t) for t in range(4)])
    for q in range(4):
        w = wide[:, q * quarter : (q + 1) * quarter]
        m = miss[0:1, q * quarter : (q + 1) * quarter]
        r = iota((8, quarter), 0)
        first = jnp.where(r == 0, m, jnp.where(r == 1, w[0:1], jnp.where(r == 2, w[1:2], 0.0)))
        second = jnp.where(r == 0, m, jnp.where(r == 1, w[2:3], jnp.where(r == 2, w[3:4], 0.0)))
        keep[q, pl.ds(2 * quarter, EXTRA), :] = first
        send[q, pl.ds(2 * quarter, EXTRA), :] = second

    def shapes(q, carry):
        arrival(q).wait()
        for half in range(2):
            rows = pl.ds(pl.multiple_of(q * quarter + half * 64, 64), 64)
            cb = table[rows, :]
            gs = [None] * 4
            for c in range(channels):
                wt = wgt[c, rows, :]
                for k in range(4):
                    term = cb[:, k * KPAD + c : k * KPAD + c + 1] * wt
                    gs[k] = term if c == 0 else gs[k] + term
            for k2 in range(2):
                keep[q, pl.ds(k2 * quarter + half * 64, 64), :] = gs[k2]
                send[q, pl.ds(k2 * quarter + half * 64, 64), :] = gs[k2 + 2]
        return carry

    lax.fori_loop(0, 4, shapes, 0)


def product_kernel(own, other, wgt_far, per_block, wgt, sems):
    channels, blocks, _ = wgt.shape
    lane = iota((128, 128), 1)
    arrival = tile_copies(wgt_far, wgt, sems)
    started([arrival(t) for t in range(blocks // 128)])

    def tile(t, carry):
        arrival(t).wait()
        rows = pl.ds(pl.multiple_of(t * 128, 128), 128)
        sh = [own[0, rows, :], own[1, rows, :], other[0, rows, :], other[1, rows, :]]
        pb = jnp.zeros((128, 128), F32)
        for c in range(channels):
            wt = wgt[c, rows, :]
            for k in range(4):
                r = jnp.sum(sh[k] * wt, axis=1, keepdims=True)
                pb = jnp.where(lane == k * KPAD + c, r, pb)
        per_block[rows, :] = pb
        return carry

    lax.fori_loop(0, blocks // 128, tile, 0)


def merge_kernel(arrived, keep, came, sent, p0, p1, p2, p3, scat):
    x, _ = band_place()
    peers = sent.shape[2]
    quarter = (p0.shape[0] - EXTRA) // 2
    blocks = 4 * quarter
    put = blocks_by_slot(sent[0], blocks)
    for k2 in range(2):
        rows = [arrived[pl.ds(k2 * 4 + j, peers, stride=ROWS), :] for j in range(4)]
        scat[k2] = pick(put, jnp.concatenate(rows, axis=0))
    for step, out in enumerate((p0, p1, p2, p3)):
        q = lax.rem(x + step, 4)
        out[...] = keep[q] + came[q]
        for k2 in range(2):
            at = pl.ds(pl.multiple_of(q * quarter, quarter), quarter)
            out[pl.ds(k2 * quarter, quarter), :] += scat[k2, at, :]


def colour_kernel(
    last, arrived, sent, per_block, lengths, own, other, colour, alive, *outs
):
    if last:
        out, fresh = outs
    else:
        fresh, table = outs
    blocks = per_block.shape[0]
    peers = sent.shape[2]
    member = membership_of(lengths[...], blocks)
    put = blocks_by_slot(sent[0], blocks)
    lane = iota((peers, 128), 1)
    rows = []
    for j in range(4):
        row = arrived[pl.ds(8 + j % 2, peers, stride=ROWS), :]
        rows.append(jnp.where((lane < 64) == (j < 2), row, 0.0))
    total = per_block[...] + pick(put, jnp.concatenate(rows, axis=0))
    hi, lo = halves(total)
    grad = lax.dot_general(hi, member, TN, preferred_element_type=F32) + lax.dot_general(
        lo, member, TN, preferred_element_type=F32
    )
    grad = grad[:64] + grad[64:]
    ones = jnp.ones((8, own.shape[2]), F32)
    for k in range(4):
        s = own[k] if k < 2 else other[k - 2]
        by_block = exact(ones, s * s, NT)
        hi, lo = halves(by_block)
        power = lax.dot_general(hi, member, NN, preferred_element_type=F32) + lax.dot_general(
            lo, member, NN, preferred_element_type=F32
        )
        step = 1.0 / (1.0 + power[:1])
        at = pl.ds(k * KPAD, KPAD)
        new = (
            jnp.maximum(colour[at, :] - step * grad[k * KPAD : (k + 1) * KPAD], 0.0)
            * alive[k : k + 1, :]
        )
        fresh[at, :] = new
    if last:
        _, h = band_place()
        for c in range(out.shape[0]):
            for k in range(4):
                out[c, pl.ds(k ^ (2 * h), 1), :] = fresh[pl.ds(k * KPAD + c, 1), :]
    else:
        table[...] = colour_table(member, fresh[...])


def update_kernel(p0, r1, r2, r3, own, ablk, out):
    x, _ = band_place()
    quarter = (p0.shape[0] - EXTRA) // 2
    total = p0[...] + r1[...] + r2[...] + r3[...]
    at = pl.ds(pl.multiple_of(x * quarter, quarter), quarter)
    ab = ablk[at, :]
    eye = iota((quarter, quarter), 0) == iota((quarter, quarter), 1)
    for k2 in range(2):
        row = total[2 * quarter + 1 + k2 : 2 * quarter + 2 + k2]
        power = jnp.sum(jnp.where(eye, row, 0.0), axis=1, keepdims=True)
        step = 1.0 / (1.0 + power)
        g = total[k2 * quarter : (k2 + 1) * quarter]
        out[pl.ds(k2 * quarter, quarter), :] = (
            jnp.maximum(own[k2, at, :] - step * g, 0.0) * ab[:, k2 : k2 + 1]
        )
    out[pl.ds(2 * quarter, EXTRA), :] = total[2 * quarter :]


def leave_kernel(n0, r1, r2, r3, table, sent, pair, message_far, message):
    x, _ = band_place()
    quarter = (n0.shape[0] - EXTRA) // 2
    for step, piece in enumerate((n0, r1, r2, r3)):
        q = lax.rem(x + 4 - step, 4)
        at = pl.ds(pl.multiple_of(q * quarter, quarter), quarter)
        for k2 in range(2):
            pair[k2, at, :] = piece[pl.ds(k2 * quarter, quarter), :]
    take = slots_by_block(sent[0], 4 * quarter)
    write_message(message, [pick(take, pair[0]), pick(take, pair[1])], pick(take, table[...]))
    pltpu.sync_copy(message, message_far)


def finish_kernel(n0, r1, r2, r3, m0, m1, m2, m3, lengths, shape, misfit):
    x, h = band_place()
    quarter = (n0.shape[0] - EXTRA) // 2
    total = jnp.zeros((8, lengths.shape[1]), F32)
    for step, (mine, theirs) in enumerate(((n0, m0), (r1, m1), (r2, m2), (r3, m3))):
        q = lax.rem(x + 4 - step, 4)
        at = pl.ds(pl.multiple_of(q * quarter, quarter), quarter)
        for k2 in range(2):
            shape[k2 + 2 * h, at, :] = mine[pl.ds(k2 * quarter, quarter), :]
            shape[k2 + 2 * (1 - h), at, :] = theirs[pl.ds(k2 * quarter, quarter), :]
        ms = mine[pl.ds(2 * quarter, EXTRA), :]
        part = membership_of(lengths[...], quarter, q * quarter)
        hi, lo = halves(ms)
        total = total + lax.dot_general(hi, part, NN, preferred_element_type=F32)
        total = total + lax.dot_general(lo, part, NN, preferred_element_type=F32)
    misfit[...] = total[:1]


def call(kernel, outs, args, scratch=(), limit=54_000_000, cost=3e6, far_in=(), far_out=()):
    many = isinstance(outs, list)
    shapes = [
        s if isinstance(s, jax.ShapeDtypeStruct) else jax.ShapeDtypeStruct(s, F32)
        for s in (outs if many else [outs])
    ]
    near = pl.BlockSpec(memory_space=pltpu.VMEM)
    far = pl.BlockSpec(memory_space=pltpu.HBM)
    got = pl.pallas_call(
        kernel,
        out_shape=shapes,
        in_specs=[far if i in far_in else near for i in range(len(args))],
        out_specs=[far if i in far_out else near for i in range(len(shapes))],
        scratch_shapes=list(scratch),
        compiler_params=pltpu.CompilerParams(vmem_limit_bytes=limit),
        cost_estimate=pl.CostEstimate(flops=0, bytes_accessed=int(cost), transcendentals=0),
    )(*args)
    return got if many else got[0]


def on_device(
    observed, weights, morphology, spectra, blend_blocks, source_count, sent_blocks, landing_blocks
):
    channels, blocks, pixels = observed.shape
    spectra = spectra.transpose(1, 0, 2)
    sent_blocks = sent_blocks.transpose(0, 2, 1)
    landing_blocks = landing_blocks.transpose(0, 2, 1)
    blends = spectra.shape[2]
    peers = sent_blocks.shape[2]
    slots = 4 * peers
    quarter = blocks // 4
    piece = (2 * quarter + EXTRA, pixels)
    pair = (2, blocks, pixels)
    message = (peers * ROWS, pixels)
    band = lax.axis_size("band")

    def over_core(v):
        return lax.ppermute(v, "band", [(i, i ^ 1) for i in range(band)])

    def over_x(v, step):
        return lax.ppermute(v, "band", [(i, (i + 2 * step) % band) for i in range(band)])

    def over_tile(v):
        v = v.reshape(peers, ROWS // 2, 2, pixels)
        return lax.all_to_all(v, "tile", 0, 0, tiled=True).reshape(message)

    counts = source_count.reshape(1, blends)
    colour_rows = (4 * KPAD, blends)
    table_rows = (blocks, 128)

    def kept(v):
        return jax.ShapeDtypeStruct(v.shape, v.dtype)

    def dma(n):
        return pltpu.SemaphoreType.DMA((n,))

    cube = pltpu.VMEM(observed.shape, F32)
    leaving = call(
        first_kernel,
        message,
        (morphology, spectra, blend_blocks, counts, sent_blocks),
        scratch=(
            pltpu.VMEM(pair, F32),
            pltpu.VMEM(spectra.shape, F32),
            pltpu.VMEM(blend_blocks.shape, jnp.int32),
            pltpu.VMEM(counts.shape, jnp.int32),
            pltpu.VMEM(sent_blocks.shape, jnp.int32),
            pltpu.VMEM(colour_rows, F32),
            pltpu.VMEM(message, F32),
            dma(5),
        ),
        limit=67_043_328,
        far_in=range(5),
        far_out=(0,),
    )
    tiles = blocks // 128
    own, other, colour, alive, table, ablk, lengths, sent, land, wide, resid = call(
        start_kernel,
        [
            pair,
            pair,
            colour_rows,
            (8, blends),
            table_rows,
            table_rows,
            kept(blend_blocks),
            kept(sent_blocks),
            kept(landing_blocks),
            (8, blocks),
            observed.shape,
        ],
        (
            morphology,
            spectra,
            blend_blocks,
            counts,
            sent_blocks,
            landing_blocks,
            observed,
        ),
        scratch=(
            pltpu.VMEM(pair, F32),
            pltpu.VMEM(pair, F32),
            pltpu.VMEM(colour_rows, F32),
            pltpu.VMEM((8, blends), F32),
            pltpu.VMEM(table_rows, F32),
            pltpu.VMEM(table_rows, F32),
            pltpu.VMEM(blend_blocks.shape, jnp.int32),
            pltpu.VMEM(sent_blocks.shape, jnp.int32),
            pltpu.VMEM(landing_blocks.shape, jnp.int32),
            pltpu.VMEM((8, blocks), F32),
            pltpu.VMEM(morphology.shape, F32),
            pltpu.VMEM(spectra.shape, F32),
            pltpu.VMEM(counts.shape, jnp.int32),
            cube,
            cube,
            dma(6),
            dma(tiles),
            dma(tiles),
            dma(10),
        ),
        cost=20e6,
        limit=67_043_328,
        far_in=range(7),
        far_out=range(11),
    )
    for iteration in range(ITERS):
        last = iteration == ITERS - 1
        mine = over_tile(leaving)
        if iteration:
            wide, resid = call(
                model_kernel,
                [(8, blocks), observed.shape],
                (table, own, other, colour, lengths, observed),
                scratch=(cube, cube, dma(tiles), dma(tiles)),
                cost=16e6,
                far_in=(5,),
                far_out=(1,),
            )
        mine, resid = lax.optimization_barrier((mine, resid))
        partner = over_core(mine)
        wgt, bkeep, bsend, miss = call(
            functools.partial(link_kernel, last),
            [observed.shape, message, message, (8, blocks)],
            (mine, partner, resid, weights, land),
            scratch=(
                pltpu.VMEM((4, slots, pixels), F32),
                pltpu.VMEM((4, slots, pixels), F32),
                pltpu.VMEM((blocks, slots), BF16),
                pltpu.VMEM((slots, blocks), BF16),
                pltpu.VMEM((blocks, pixels), F32),
                cube,
                cube,
                cube,
                dma(channels),
                dma(channels),
                dma(channels),
            ),
            cost=14e6,
            far_in=(2, 3),
            far_out=(0,),
        )
        returning = bkeep + over_core(bsend)
        back = over_tile(returning)
        gkeep, gsend = call(
            grad_kernel,
            [(4,) + piece, (4,) + piece],
            (table, wgt, wide, miss, returning),
            scratch=(cube, dma(tiles)),
            cost=16e6,
            far_in=(1, 4),
        )
        gcame = over_core(gsend)
        p0, p1, p2, p3 = call(
            merge_kernel,
            [piece] * 4,
            (back, gkeep, gcame, sent),
            scratch=(pltpu.VMEM(pair, F32),),
            limit=SMALL,
        )
        r1, r2, r3 = (over_x(v, s) for s, v in ((1, p1), (2, p2), (3, p3)))
        per_block = call(
            product_kernel,
            table_rows,
            (own, other, wgt),
            scratch=(cube, dma(tiles)),
            cost=16e6,
            far_in=(2,),
        )
        colour_args = (back, sent, per_block, lengths, own, other, colour, alive)
        if last:
            new_colour = call(
                functools.partial(colour_kernel, True),
                (channels, 4, blends),
                colour_args,
                scratch=(pltpu.VMEM(colour_rows, F32),),
                limit=SMALL,
                cost=8e6,
            )
        else:
            colour, table = call(
                functools.partial(colour_kernel, False),
                [colour_rows, table_rows],
                colour_args,
                limit=SMALL,
                cost=8e6,
            )
        n0 = call(update_kernel, piece, (p0, r1, r2, r3, own, ablk), limit=SMALL)
        n1, n2, n3 = (over_x(n0, s) for s in (1, 2, 3))
        if not last:
            own, leaving = call(
                leave_kernel, [pair, message], (n0, n1, n2, n3, table, sent),
                scratch=(pltpu.VMEM(message, F32),),
                limit=SMALL,
                far_out=(1,),
            )
            other = over_core(own)
    m0, m1, m2, m3 = (over_core(v) for v in (n0, n1, n2, n3))
    shape, misfit = call(
        finish_kernel,
        [morphology.shape, (1, blends)],
        (n0, n1, n2, n3, m0, m1, m2, m3, lengths),
        limit=SMALL,
    )
    return shape, new_colour.transpose(1, 0, 2), misfit.reshape(blends)


def solution(mesh):
    return jax.shard_map(
        on_device,
        mesh=mesh,
        in_specs=(
            P("band", "tile", None),
            P("band", "tile", None),
            P(None, "tile", None),
            P(None, "band", "tile"),
            P("tile", None),
            P("tile"),
            P("tile", None, None),
            P("tile", None, None),
        ),
        out_specs=(P(None, "tile", None), P(None, "band", "tile"), P("tile")),
        check_vma=False,
    )
```
